32 devices in a mesh: grp: 2 (over y), tgt: 4 (over z), src: 4 (over x, core).
Axes of the slice: x: 2, y: 2, z: 4, core: 2. Of those that a mesh axis runs over, the one named last changes fastest.
Arguments:
- target_rows: bfloat16 [2048, 4608], P(('grp', 'tgt', 'src')), parts along dimension 0, may hold values from -6 to 6
- target_pos: int32 [2048], P(('grp', 'tgt')), parts along dimension 0, may hold values from 0 to 255
- decoder_rows: bfloat16 [512, 4608], P(('grp', 'tgt', 'src')), parts along dimension 0, may hold values from -0.09375 to 0.09375
- source_pos: int32 [512], P('grp'), parts along dimension 0, may hold values from 0 to 255
- out_proj: bfloat16 [32, 4608, 128], P('src', 'tgt'), may hold values from -0.09375 to 0.09375
- value_proj: bfloat16 [16, 4608, 128], P('src'), may hold values from -1 to 1
- attention: bfloat16 [64, 256, 256], P(('grp', 'src'), 'tgt'), parts along dimension 0, may hold values from 0 to 1, as said below
- tile_pattern: int32 [8, 4], P('grp'), parts along dimension 0, may hold values from 0 to 1, as said below
Outputs:
- edges: bfloat16 [512, 1024], P(('grp', 'src'), 'tgt'), parts along dimension 0
The draws below stay inside these ranges and needn't reach their ends.
There are 2 independent parts, one for each index of `grp`. The reference program is written for one: setup_inputs(seed, part) draws one part's arguments, and reference() takes and returns one part's arrays. A program takes and returns all parts, laid end to end along the dimension named above; an argument that names none is the same for every part. Nothing has to cross between parts.
Inputs may be any that keep to these rules, and one draw needn't show every extreme that they name: Each row attention[h, p, :] is a probability distribution over the keys 0 to p: zero beyond p, summing to one. tile_pattern[b, c] is 1 where the tile of edges between source block b and target block c is kept, else 0.
All inputs are finite; a program needn't handle non-finite values.
Results may differ from the reference program's by a relative error of at most 0.0057.
Values may be sent and summed in bfloat16 or wider, within the bound.
No kernel may reach another device: no remote copies, remote signals or barrier semaphores. Data moves between devices by JAX's collectives and lax.ppermute only.
A program may use at most 64 MiB of HBM per device.

```python
import jax
import jax.numpy as jnp
from jax import lax

D = 4608
H = 32
KV = 16
HD = 128
S = 256
TGT_DEV = 256
SRC_DEV = 64
BLOCKS = 4
NT = 1024
NS = 256


def draw_attention(key, part):
    noise_key = jax.random.fold_in(key, 11)
    logits = 3.0 * jax.random.normal(noise_key, (H, S, S), jnp.float32)
    query_pos = jnp.arange(S)[:, None]
    key_pos = jnp.arange(S)[None, :]
    causal = key_pos <= query_pos
    logits = jnp.where(causal[None], logits, -1e+30)
    weights = jax.nn.softmax(logits, axis=-1)
    return weights.astype(jnp.bfloat16)


def draw_tile_pattern(key, part):
    level_key, roll_key = jax.random.split(jax.random.fold_in(key, 23))
    levels = jnp.array([6, 12, 25, 50, 100], jnp.int32)
    choose = jax.random.randint(level_key, (BLOCKS,), 0, 5)
    dice_rolls = jax.random.randint(roll_key, (BLOCKS, BLOCKS), 0, 100)
    return (dice_rolls < levels[choose][None, :]).astype(jnp.int32)


def touch_ends(entries, rng, smallest, top_value):
    longest = entries.shape.index(max(entries.shape))
    spots = []
    for shift in (0, 1):
        where = [jax.random.randint(jax.random.fold_in(rng, axis), (), 0, length) for axis, length in enumerate(entries.shape)]
        where[longest] = (where[longest] + shift) % entries.shape[longest]
        spots.append(tuple(where))
    return entries.at[spots[0]].set(smallest).at[spots[1]].set(top_value)


def block_levels(key, shape, cuts, low, high):
    level = 1.0
    for position, shards_of in cuts:
        steps = jax.random.uniform(jax.random.fold_in(jax.random.fold_in(key, 6), position), (shards_of,), jnp.float32, low / len(cuts), high / len(cuts))
        level = level * jnp.repeat(jnp.exp(steps), shape[position] // shards_of).reshape((-1,) + (1,) * (len(shape) - 1 - position))
    return level


def centred(stream_key, shape, deviation, most, pieces=(), held_as=jnp.bfloat16):
    result = deviation * jax.random.normal(stream_key, shape, jnp.float32)
    if pieces:
        result = result * block_levels(stream_key, shape, pieces, -0.22, 0.18)
    return jnp.clip(result, -most, most).astype(held_as)


def setup_inputs(seed: int = 0, part: int = 0) -> dict:
    key_of = jax.random.split(jax.random.key(seed), 9)
    part_keys = jax.random.split(jax.random.fold_in(key_of[8], part), 9)
    return {
        "target_rows": centred(part_keys[0], (NT, D), 1.0, 6.0, ((0, 16),)),
        "target_pos": touch_ends(jax.random.randint(part_keys[1], (NT,), 0, S), jax.random.fold_in(part_keys[1], 1), 0, S - 1).astype(jnp.int32),
        "decoder_rows": centred(part_keys[2], (NS, D), D ** -0.5, 0.09375, ((0, 16),)),
        "source_pos": touch_ends(jax.random.randint(part_keys[3], (NS,), 0, S), jax.random.fold_in(part_keys[3], 1), 0, S - 1).astype(jnp.int32),
        "out_proj": centred(key_of[4], (H, D, HD), D ** -0.5, 0.09375, ((0, 4), (1, 4))),
        "value_proj": centred(key_of[5], (KV, D, HD), (HD // 4) ** -0.5, 1.0, ((0, 4),)),
        "attention": draw_attention(jax.random.fold_in(jax.random.fold_in(key_of[8], part), 71), part),
        "tile_pattern": draw_tile_pattern(jax.random.fold_in(jax.random.fold_in(key_of[8], part), 71), part),
    }


def reference(target_rows, target_pos, decoder_rows, source_pos, out_proj, value_proj, attention, tile_pattern):
    highest = lax.Precision.HIGHEST
    targets_wide = target_rows.astype(jnp.float32)
    sources_wide = decoder_rows.astype(jnp.float32)
    head_reads = jnp.einsum('td,hde->the', targets_wide, out_proj.astype(jnp.float32), precision=highest).astype(jnp.bfloat16)
    source_values = jnp.einsum('nd,gde->nge', sources_wide, value_proj.astype(jnp.float32), precision=highest).astype(jnp.bfloat16)
    same_place = (source_pos[:, None] == target_pos[None, :]).astype(jnp.float32)
    direct = jnp.dot(sources_wide, targets_wide.T, precision=highest) * same_place
    repeat = H // KV

    def add_head(head_index, running):
        group_index = head_index // repeat
        value_part = lax.dynamic_index_in_dim(source_values, group_index, 1, keepdims=False).astype(jnp.float32)
        read_part = lax.dynamic_index_in_dim(head_reads, head_index, 1, keepdims=False).astype(jnp.float32)
        scores = jnp.dot(value_part, read_part.T, precision=highest)
        attn_table = lax.dynamic_index_in_dim(attention, head_index, 0, keepdims=False).astype(jnp.float32)
        weights = jnp.take(jnp.take(attn_table, target_pos, axis=0), source_pos, axis=1).T
        return running + weights * scores

    mixed_term = lax.fori_loop(0, H, add_head, jnp.zeros((NS, NT), jnp.float32))
    keep_mask = jnp.repeat(jnp.repeat(tile_pattern, SRC_DEV, axis=0), TGT_DEV, axis=1).astype(jnp.float32)
    return (keep_mask * (direct + mixed_term)).astype(jnp.bfloat16)
```

```python
import functools

import jax
import jax.numpy as jnp
from jax import lax
from jax.experimental import pallas as pl
from jax.experimental.pallas import tpu as pltpu
from jax.sharding import PartitionSpec as P

F32 = jnp.float32
BF16 = jnp.bfloat16
VMEM_BYTES = 48 << 20


def passed_along(value, axis, steps):
    count = lax.axis_size(axis)
    pairs = [(source, (source + steps) % count) for source in range(count)]
    return lax.ppermute(value, axis, pairs)


def swapped(value, axis, bit):
    pairs = [(source, source ^ bit) for source in range(lax.axis_size(axis))]
    return lax.ppermute(value, axis, pairs)


def kernel_call(body, outs, grid, in_specs, out_specs, scratch, scalars, args, flops, moved):
    return pl.pallas_call(
        body,
        out_shape=outs,
        grid_spec=pltpu.PrefetchScalarGridSpec(
            num_scalar_prefetch=1,
            grid=grid,
            in_specs=in_specs,
            out_specs=out_specs,
            scratch_shapes=scratch,
        ),
        compiler_params=pltpu.CompilerParams(
            dimension_semantics=("arbitrary",) * len(grid), vmem_limit_bytes=VMEM_BYTES
        ),
        cost_estimate=pl.CostEstimate(flops=flops, bytes_accessed=moved, transcendentals=0),
    )(scalars, *args)


def whole(array, rows=None):
    shape = array.shape if rows is None else (rows,) + array.shape[1:]
    return pl.BlockSpec(shape, lambda *_: (0,) * len(shape))


def pair_of(ref, first):
    return jnp.concatenate([ref[first], ref[first + 1]], axis=-1)


def payload_kernel(rows, lane, own, core, far, cross, value, attn, spos, tpos, out, total):
    step = pl.program_id(0)
    subs = own.shape[0] - rows
    sub = subs // pl.num_programs(0)
    heads, queries, keys = attn.shape
    groups = value.shape[0]
    sources = spos.shape[1]
    base = heads * queries
    block = 4 * sub

    @pl.when(step == 0)
    def _():
        total[...] = jnp.zeros_like(total)
        picks = lax.broadcasted_iota(jnp.int32, (keys, sources), 0) == spos[...]
        picks = picks.astype(F32).astype(BF16)
        table = attn[...].reshape(base, keys)
        out[0:base, :] = jnp.dot(table, picks, preferred_element_type=F32).astype(BF16)
        tail = out.shape[0] - base - block * (groups // 2)
        out[out.shape[0] - tail :, :] = jnp.broadcast_to(
            tpos[...].astype(F32), (tail, tpos.shape[1])
        ).astype(BF16)

    at = pl.ds(pl.multiple_of(rows + step * sub, sub), sub)
    left = jnp.concatenate([own[at, :], core[at, :], far[at, :], cross[at, :]], axis=0)
    for pair in range(groups // 2):
        cols = slice(pair * sources, (pair + 1) * sources)
        total[:, cols] += jnp.dot(left, pair_of(value, 2 * pair), preferred_element_type=F32)

    @pl.when(step == pl.num_programs(0) - 1)
    def _():
        for pair in range(groups // 2):
            cols = slice(pair * sources, (pair + 1) * sources)
            for j in range(4):
                spot = pl.multiple_of(base + pair * block + lane[j] * sub, sub)
                out[pl.ds(spot, sub), :] = total[j * sub : (j + 1) * sub, cols].astype(BF16)


def reads_kernel(rows, info, own, core, far, cross, first, second, third, fourth, weight, reads, direct, dec):
    sub = second.shape[0] - rows
    dec[...] = jnp.zeros_like(dec)
    for k, ref in enumerate((first, second, third, fourth)):
        if k:
            piece = ref[rows:, :]
        else:
            piece = ref[pl.ds(pl.multiple_of(info[8], sub), sub), :]
        dec[pl.ds(pl.multiple_of(info[4 + k], sub), sub), :] = piece
    left = jnp.concatenate([ref[0:rows, :] for ref in (own, core, far, cross)], axis=0)
    width = 2 * weight.shape[2]

    def put(target, cols, value):
        for j in range(4):
            spot = pl.multiple_of(info[j] * rows, rows)
            target[pl.ds(spot, rows), cols] = value[j * rows : (j + 1) * rows].astype(target.dtype)

    for pair in range(weight.shape[0] // 2):
        got = jnp.dot(left, pair_of(weight, 2 * pair), preferred_element_type=F32)
        put(reads, slice(pair * width, (pair + 1) * width), got)
    put(
        direct,
        slice(0, direct.shape[1]),
        lax.dot_general(left, dec[...], (((1,), (1,)), ((), ())), preferred_element_type=F32),
    )


def edges_kernel(heads, queries, info, *refs):
    home, right1, right2, right3, left1, left2, left3 = refs[:7]
    reads = refs[7:11]
    direct = refs[11:15]
    spos, out, table, values = refs[15:]
    sources = spos.shape[1]
    half = sources // 2
    base = heads * queries
    block = sources // 4
    wide = 2 * (reads[0].shape[1] // heads)
    dim = wide // 2
    pairs = heads // 2
    here = info[8]
    table[0] = home[...]
    for k, (near, other) in enumerate(((right1, left3), (right2, left2), (right3, left1)), 1):

        @pl.when(here >= k)
        def _(k=k, near=near):
            table[k] = near[...]

        @pl.when(here < k)
        def _(k=k, other=other):
            table[k] = other[...]

    for k in range(4):
        for p in range(pairs // 2):
            values[pl.ds(pl.multiple_of(info[4 + k], block), block), p * sources : (p + 1) * sources] = (
                table[k, base + p * block : base + (p + 1) * block, :]
            )
    lanes = pl.ds(pl.multiple_of(info[9] * half, half), half)
    spot = pl.multiple_of(info[9] * half, half)
    grid_q = jnp.concatenate(
        [lax.broadcasted_iota(jnp.int32, (queries, sources), 0) + info[k] for k in range(4)], axis=0
    )
    picks = (grid_q[:, :half] == spos[:, lanes]).astype(F32).astype(BF16)
    blank = jnp.zeros((dim, half), BF16)
    scorers, tables = [], []
    for pair in range(pairs):
        turned = values[pl.ds(spot, half), pair * dim : (pair + 1) * dim].astype(F32).T.astype(BF16)
        scorers.append(
            jnp.concatenate(
                [
                    jnp.concatenate([turned, blank], axis=1),
                    jnp.concatenate([blank, turned], axis=1),
                ],
                axis=0,
            )
        )
        tables.append(
            jnp.concatenate(
                [
                    jnp.concatenate(
                        [table[k, h * queries : (h + 1) * queries, lanes] for k in range(4)], axis=0
                    )
                    for h in (2 * pair, 2 * pair + 1)
                ],
                axis=1,
            )
        )
    for k in range(4):
        tpos = table[k, table.shape[1] - 16 : table.shape[1], :].astype(F32)[0:1].astype(jnp.int32)
        hot = (grid_q == tpos).astype(F32).T.astype(BF16)
        running = None
        for pair in range(pairs):
            weights = jnp.dot(hot, tables[pair], preferred_element_type=F32)
            scores = jnp.dot(
                reads[k][:, pair * wide : (pair + 1) * wide], scorers[pair], preferred_element_type=F32
            )
            term = weights * scores
            running = term if running is None else running + term
        mixed = running[:, :half] + running[:, half:]
        same = jnp.dot(hot, picks, preferred_element_type=F32)
        turned = (mixed + same * direct[k][:, lanes]).T
        cols = slice(k * sources, (k + 1) * sources)
        for side in range(2):
            row = pl.multiple_of(info[10 + side], block)
            out[pl.ds(row, block), cols] = turned[side * block : (side + 1) * block, :]


def resident(
    target_rows, target_pos, decoder_rows, source_pos, out_proj, value_proj, attention, tile_pattern
):
    blocks = lax.axis_size("tgt")
    z = lax.axis_index("tgt")
    s = lax.axis_index("src")
    rows, depth = target_rows.shape
    sub = decoder_rows.shape[0]
    part = depth // blocks
    heads, _, head_dim = out_proj.shape
    groups = value_proj.shape[0]
    queries = attention.shape[1]
    sources = source_pos.shape[0]
    targets = target_pos.shape[0]
    block = sources // blocks
    ks = jnp.arange(4, dtype=jnp.int32)
    lane = s ^ ks
    origin = (z - ks) % blocks
    source_spot = (origin % 2) * (2 * block) + (origin // 2) * block

    stacked = [decoder_rows[:, i * part : (i + 1) * part] for i in range(blocks)]

    def piece(array, column):
        return lax.dynamic_slice_in_dim(array, column * part, part, 1)

    outgoing = [
        jnp.concatenate([piece(target_rows, (z + k) % blocks), piece(decoder_rows, (z + k) % blocks)], 0)
        for k in range(1, blocks)
    ]
    own = [jnp.concatenate([piece(target_rows, z)] + stacked, 0)]
    own += [passed_along(outgoing[k - 1], "tgt", k) for k in range(1, blocks)]
    far = [swapped(value, "src", 2) for value in own]
    core = [swapped(value, "src", 1) for value in own]
    cross = [swapped(value, "src", 1) for value in far]

    ordered = source_pos.reshape(2, 2, block).transpose(1, 0, 2).reshape(1, sources)
    tall = heads * queries + block * (groups // 2) + 16
    home = kernel_call(
        functools.partial(payload_kernel, rows),
        jax.ShapeDtypeStruct((tall, sources), BF16),
        (blocks,),
        [whole(own[0])] * 4
        + [
            pl.BlockSpec((groups, part, head_dim), lambda i, _: (0, i, 0)),
            whole(attention),
            whole(ordered),
            pl.BlockSpec((1, targets), lambda *_: (0, 0)),
        ],
        pl.BlockSpec((tall, sources), lambda *_: (0, 0)),
        [pltpu.VMEM((4 * sub, groups * head_dim), F32)],
        lane,
        [own[0], core[0], far[0], cross[0], value_proj, attention, ordered, target_pos[None, :]],
        2 * 4 * sub * depth * groups * head_dim,
        value_proj.size * 2,
    )
    rightward, leftward = [home], [home]
    for step in range(1, blocks):
        up = [(i, i + 1) for i in range(step - 1, blocks - 1)]
        down = [(blocks - 1 - i, blocks - 2 - i) for i in range(step - 1, blocks - 1)]
        rightward.append(lax.ppermute(rightward[-1], "tgt", up))
        leftward.append(lax.ppermute(leftward[-1], "tgt", down))

    info = jnp.concatenate([lane, source_spot + sub * s, (rows + sub * z)[None]]).astype(jnp.int32)
    reads, direct = [], []
    for k in range(blocks):
        got = kernel_call(
            functools.partial(reads_kernel, rows),
            (
                jax.ShapeDtypeStruct((4 * rows, heads * head_dim), BF16),
                jax.ShapeDtypeStruct((4 * rows, sources), F32),
            ),
            (1,),
            [whole(own[k], rows)] * 4 + [whole(a) for a in own] + [whole(out_proj)],
            (
                pl.BlockSpec((4 * rows, heads * head_dim), lambda *_: (0, 0)),
                pl.BlockSpec((4 * rows, sources), lambda *_: (0, 0)),
            ),
            [pltpu.VMEM((sources, part), BF16)],
            info,
            [own[k], core[k], far[k], cross[k], *own, out_proj],
            2 * 4 * rows * part * (heads * head_dim + sources),
            out_proj.size * 2,
        )
        reads.append(got[0])
        direct.append(got[1])

    def edges(side):
        x = s // 2
        places = jnp.where(jnp.arange(2) == x, block, 0)
        facts = jnp.concatenate([origin * queries, source_spot, z[None], side[None], places])
        args = [home, *rightward[1:], *leftward[1:], *reads, *direct, ordered]
        return kernel_call(
            functools.partial(edges_kernel, heads, queries),
            jax.ShapeDtypeStruct((sources // 2, blocks * targets), F32),
            (1,),
            [whole(a) for a in args],
            pl.BlockSpec((sources // 2, blocks * targets), lambda *_: (0, 0)),
            [
                pltpu.VMEM((4,) + home.shape, BF16),
                pltpu.VMEM((sources, groups * head_dim), BF16),
            ],
            facts.astype(jnp.int32),
            args,
            2 * 2 * blocks * targets * sources * heads * head_dim,
            1 << 22,
        )

    side = s % 2
    away = swapped(edges(1 - side), "src", 1)
    kept = edges(side)
    sent = (kept[:block] + away[:block]).astype(BF16)
    back = swapped(sent, "src", 2)
    mine = kept[block:] + away[block:] + back.astype(F32)
    result = mine[:, :targets]
    for k in range(1, blocks):
        result = result + passed_along(
            mine[:, k * targets : (k + 1) * targets].astype(BF16), "tgt", -k
        ).astype(F32)
    return (result * tile_pattern[s, z].astype(F32)).astype(BF16)


def ring(
    target_rows, target_pos, decoder_rows, source_pos, out_proj, value_proj, attention, tile_pattern
):
    blocks = lax.axis_size("tgt")
    column = lax.axis_index("tgt")
    src_lane = lax.axis_index("src")
    full_targets, full_sources = (
        lax.all_gather(target_rows, "src", axis=0, tiled=True),
        lax.all_gather(decoder_rows, "src", axis=0, tiled=True),
    )
    tgt_dev = full_targets.shape[0]
    src_dev = full_sources.shape[0]
    sub_rows = decoder_rows.shape[0]
    heads_here = out_proj.shape[0]
    head_dim = out_proj.shape[2]
    groups_here = value_proj.shape[0]
    repeat = heads_here // groups_here
    read_sum = jnp.einsum(
        "td,hde->the",
        full_targets,
        lax.all_gather(out_proj, "tgt", axis=1, tiled=True),
        preferred_element_type=jnp.float32,
    )
    head_reads = read_sum.astype(jnp.bfloat16).reshape(tgt_dev, groups_here, repeat, head_dim)
    values = jnp.einsum("sd,gde->sge", full_sources, value_proj, preferred_element_type=jnp.float32)
    values = values.astype(jnp.bfloat16).reshape(src_dev, groups_here * head_dim)
    attn_table = lax.all_gather(attention, "tgt", axis=1, tiled=True)
    target_attn = jnp.take(attn_table, target_pos, axis=1)
    keyed_attn = jnp.transpose(target_attn, (0, 2, 1))

    def edge_tile(payload, block_index):
        decoder_part, value_part = payload
        key_positions = lax.dynamic_slice_in_dim(source_pos, block_index * src_dev, src_dev)
        weights = jnp.take(keyed_attn, key_positions, axis=1).astype(jnp.float32)
        scores = jnp.einsum(
            "sgd,tgrd->grst",
            value_part.reshape(src_dev, groups_here, head_dim),
            head_reads,
            preferred_element_type=jnp.float32,
        )
        scores = scores.reshape(heads_here, src_dev, tgt_dev)
        mixed_term = jnp.sum(weights * scores, axis=0)
        own_positions = lax.dynamic_slice_in_dim(key_positions, src_lane * sub_rows, sub_rows)
        same_place = (own_positions[:, None] == target_pos[None, :]).astype(jnp.float32)
        direct = (
            jnp.einsum("sd,td->st", decoder_part, full_targets, preferred_element_type=jnp.float32)
            * same_place
        )
        own_rows = lax.dynamic_slice_in_dim(mixed_term, src_lane * sub_rows, sub_rows, 0)
        return lax.dynamic_update_slice_in_dim(
            mixed_term, own_rows + direct, src_lane * sub_rows, 0
        )

    def place_tile(partial_value, payload, block_index):
        kept_flag = tile_pattern[block_index, column]
        piece_tile = edge_tile(payload, block_index) * kept_flag.astype(jnp.float32)
        return lax.dynamic_update_slice_in_dim(partial_value, piece_tile, block_index * src_dev, 0)

    own_block = (decoder_rows, values)
    partial_value = jnp.zeros((blocks * src_dev, tgt_dev), jnp.float32)
    partial_value = place_tile(partial_value, own_block, column)

    def cycle_turn(turn_index, state_carry):
        forward_block, backward_block, running = state_carry
        forward_block = passed_along((forward_block[0], forward_block[1]), "tgt", 1)
        backward_block = passed_along((backward_block[0], backward_block[1]), "tgt", -1)
        running = place_tile(running, forward_block, (column - turn_index) % blocks)
        running = place_tile(running, backward_block, (column + turn_index) % blocks)
        return (forward_block, backward_block, running)

    forward_block, backward_block, partial_value = lax.fori_loop(
        1, blocks // 2, cycle_turn, (own_block, own_block, partial_value)
    )
    forward_block = passed_along((forward_block[0], forward_block[1]), "tgt", 1)
    partial_value = place_tile(partial_value, forward_block, (column - blocks // 2) % blocks)
    summed = lax.psum_scatter(partial_value, "src", scatter_dimension=0, tiled=True)
    return summed.astype(jnp.bfloat16)


def shards(*args):
    target_rows, target_pos, decoder_rows, source_pos, out_proj, value_proj, attention, _ = args
    blocks, lanes = lax.axis_size("tgt"), lax.axis_size("src")
    heads, groups = out_proj.shape[0], value_proj.shape[0]
    fits = (
        blocks == 4
        and lanes == 4
        and out_proj.shape[1] % 128 == 0
        and out_proj.shape[2] == 128
        and heads == 2 * groups
        and groups % 2 == 0
        and source_pos.shape[0] == target_pos.shape[0] == attention.shape[2] == 256
        and target_rows.shape[0] % 16 == 0
        and decoder_rows.shape[0] % 16 == 0
        and attention.shape[1] % 16 == 0
    )
    return resident(*args) if fits else ring(*args)


def solution(mesh):
    return jax.shard_map(
        shards,
        mesh=mesh,
        in_specs=(
            P(("grp", "tgt", "src"), None),
            P(("grp", "tgt")),
            P(("grp", "tgt", "src"), None),
            P("grp"),
            P("src", "tgt", None),
            P("src", None, None),
            P(("grp", "src"), "tgt", None),
            P("grp", None),
        ),
        out_specs=P(("grp", "src"), "tgt"),
        check_vma=False,
    )
```

```python
import functools

import jax
import jax.numpy as jnp
from jax import lax
from jax.experimental import pallas as pl
from jax.experimental.pallas import tpu as pltpu
from jax.sharding import PartitionSpec as P

F32 = jnp.float32
BF16 = jnp.bfloat16
VMEM_BYTES = 24 << 20


def passed_along(value, axis, steps):
    count = lax.axis_size(axis)
    pairs = [(source, (source + steps) % count) for source in range(count)]
    return lax.ppermute(value, axis, pairs)


def swapped(value, axis, bit):
    pairs = [(source, source ^ bit) for source in range(lax.axis_size(axis))]
    return lax.ppermute(value, axis, pairs)


def kernel_call(body, outs, args, flops, moved, scratch=(), smem=()):
    return pl.pallas_call(
        body,
        out_shape=outs,
        in_specs=[
            pl.BlockSpec(memory_space=pltpu.SMEM if i in smem else pltpu.VMEM)
            for i in range(len(args))
        ],
        out_specs=jax.tree.map(lambda _: pl.BlockSpec(memory_space=pltpu.VMEM), outs),
        scratch_shapes=scratch,
        compiler_params=pltpu.CompilerParams(vmem_limit_bytes=VMEM_BYTES),
        cost_estimate=pl.CostEstimate(flops=flops, bytes_accessed=moved, transcendentals=0),
    )(*args)


def aligned(start, size):
    return pl.ds(pl.multiple_of(start, size), size)


def pair_of(ref, first, rows=slice(None)):
    return jnp.concatenate([ref[first, rows, :], ref[first + 1, rows, :]], axis=-1)


def origin_of(z, k):
    return jnp.where(z >= k, z - k, z - k + 4)


def source_row(z, k, block):
    b = origin_of(z, k)
    return (b % 2) * (2 * block) + (b // 2) * block


def cut_kernel(targets, sources, own, first, second, third):
    z = lax.axis_index("tgt")
    rows, sub = targets.shape[0], sources.shape[0]
    part = own.shape[1]

    def columns(index):
        return pl.ds(pl.multiple_of(index * part, 128), part)

    own[0:rows, :] = targets[:, columns(z)]
    for i in range(4):
        own[rows + i * sub : rows + (i + 1) * sub, :] = sources[:, i * part : (i + 1) * part]
    for k, out in enumerate((first, second, third), 1):
        at = columns(jnp.where(z + k >= 4, z + k - 4, z + k))
        out[0:rows, :] = targets[:, at]
        out[rows:, :] = sources[:, at]


def payload_kernel(rows, own, core, far, cross, value, attn, spos, tpos, out):
    s = lax.axis_index("src")
    sub = (own.shape[0] - rows) // 4
    part = own.shape[1]
    heads, queries, keys = attn.shape
    groups = value.shape[0]
    sources = spos.shape[1]
    base = heads * queries
    block = 4 * sub
    picks = lax.broadcasted_iota(jnp.int32, (keys, sources), 0) == spos[...]
    picks = picks.astype(F32).astype(BF16)
    table = attn[...].reshape(base, keys)
    out[0:base, :] = jnp.dot(table, picks, preferred_element_type=F32).astype(BF16)
    tail = out.shape[0] - base - block * (groups // 2)
    out[out.shape[0] - tail :, :] = jnp.broadcast_to(
        tpos[...].astype(F32), (tail, tpos.shape[1])
    ).astype(BF16)
    for pair in range(groups // 2):
        total = None
        for i in range(4):
            at = slice(rows + i * sub, rows + (i + 1) * sub)
            left = jnp.concatenate([ref[at, :] for ref in (own, core, far, cross)], axis=0)
            got = jnp.dot(
                left,
                pair_of(value, 2 * pair, slice(i * part, (i + 1) * part)),
                preferred_element_type=F32,
            )
            total = got if total is None else total + got
        for j in range(4):
            spot = base + pair * block + (s ^ j) * sub
            out[aligned(spot, sub), :] = total[j * sub : (j + 1) * sub, :].astype(BF16)


def reads_kernel(rows, *refs):
    pieces, weight, reads, direct, dec = refs[:16], refs[16], refs[17], refs[18], refs[19]
    z, s = lax.axis_index("tgt"), lax.axis_index("src")
    sub = pieces[4].shape[0] - rows
    block = 4 * sub
    dec[...] = jnp.zeros_like(dec)
    for k in range(4):
        if k:
            piece = pieces[4 * k][rows:, :]
        else:
            piece = pieces[0][aligned(rows + sub * z, sub), :]
        dec[aligned(source_row(z, k, block) + sub * s, sub), :] = piece
    width = 2 * weight.shape[2]
    group = 4 * rows

    def put(k, target, cols, value):
        for j in range(4):
            target[aligned(k * group + (s ^ j) * rows, rows), cols] = value[
                j * rows : (j + 1) * rows
            ].astype(target.dtype)

    lefts = [
        jnp.concatenate([ref[0:rows, :] for ref in pieces[4 * k : 4 * k + 4]], axis=0)
        for k in range(4)
    ]
    for pair in range(weight.shape[0] // 2):
        right = pair_of(weight, 2 * pair)
        for k in range(4):
            got = jnp.dot(lefts[k], right, preferred_element_type=F32)
            put(k, reads, slice(pair * width, (pair + 1) * width), got)
    for k in range(4):
        got = lax.dot_general(
            lefts[k], dec[...], (((1,), (1,)), ((), ())), preferred_element_type=F32
        )
        put(k, direct, slice(0, direct.shape[1]), got)


def edges_kernel(heads, queries, flip, *refs):
    home, right1, right2, right3, left1, left2, left3 = refs[:7]
    reads, direct, spos, out, table, values = refs[7:]
    z, s = lax.axis_index("tgt"), lax.axis_index("src")
    side = (s % 2) ^ flip
    sources = spos.shape[1]
    half = sources // 2
    base = heads * queries
    block = sources // 4
    wide = 2 * (reads.shape[1] // heads)
    dim = wide // 2
    pairs = heads // 2
    table[0] = home[...]
    for k, (near, other) in enumerate(((right1, left3), (right2, left2), (right3, left1)), 1):

        @pl.when(z >= k)
        def _(k=k, near=near):
            table[k] = near[...]

        @pl.when(z < k)
        def _(k=k, other=other):
            table[k] = other[...]

    for k in range(4):
        for p in range(pairs // 2):
            values[aligned(source_row(z, k, block), block), p * sources : (p + 1) * sources] = table[
                k, base + p * block : base + (p + 1) * block, :
            ]
    lanes = aligned(side * half, half)
    grid_q = jnp.concatenate(
        [
            lax.broadcasted_iota(jnp.int32, (queries, sources), 0) + origin_of(z, k) * queries
            for k in range(4)
        ],
        axis=0,
    )
    picks = (grid_q[:, :half] == spos[:, lanes]).astype(F32).astype(BF16)
    blank = jnp.zeros((dim, half), BF16)
    scorers, tables = [], []
    for pair in range(pairs):
        turned = values[lanes, pair * dim : (pair + 1) * dim].astype(F32).T.astype(BF16)
        scorers.append(
            jnp.concatenate(
                [
                    jnp.concatenate([turned, blank], axis=1),
                    jnp.concatenate([blank, turned], axis=1),
                ],
                axis=0,
            )
        )
        tables.append(
            jnp.concatenate(
                [
                    jnp.concatenate(
                        [table[k, h * queries : (h + 1) * queries, lanes] for k in range(4)], axis=0
                    )
                    for h in (2 * pair, 2 * pair + 1)
                ],
                axis=1,
            )
        )
    for k in range(4):
        tpos = table[k, table.shape[1] - 16 : table.shape[1], :].astype(F32)[0:1].astype(jnp.int32)
        hot = (grid_q == tpos).astype(F32).T.astype(BF16)
        here = slice(k * sources, (k + 1) * sources)
        running = None
        for pair in range(pairs):
            weights = jnp.dot(hot, tables[pair], preferred_element_type=F32)
            scores = jnp.dot(
                reads[here, pair * wide : (pair + 1) * wide],
                scorers[pair],
                preferred_element_type=F32,
            )
            term = weights * scores
            running = term if running is None else running + term
        mixed = running[:, :half] + running[:, half:]
        same = jnp.dot(hot, picks, preferred_element_type=F32)
        turned = (mixed + same * direct[here, lanes]).T
        for x in range(2):
            row = jnp.where(s // 2 == x, block, 0)
            out[aligned(row, block), here] = turned[x * block : (x + 1) * block, :]


def finish_kernel(pattern, mine, first, second, third, out):
    kept = pattern[lax.axis_index("src"), lax.axis_index("tgt")].astype(F32)
    total = mine[...]
    for ref in (first, second, third):
        total = total + ref[...].astype(F32)
    out[...] = (total * kept).astype(BF16)


def resident(
    target_rows, target_pos, decoder_rows, source_pos, out_proj, value_proj, attention, tile_pattern
):
    blocks = lax.axis_size("tgt")
    rows, depth = target_rows.shape
    sub = decoder_rows.shape[0]
    part = depth // blocks
    heads, _, head_dim = out_proj.shape
    groups = value_proj.shape[0]
    queries = attention.shape[1]
    sources = source_pos.shape[0]
    targets = target_pos.shape[0]
    block = sources // blocks

    def shape(*dims, dtype=BF16):
        return jax.ShapeDtypeStruct(dims, dtype)

    cut = kernel_call(
        cut_kernel,
        (shape(rows + 4 * sub, part),) + (shape(rows + sub, part),) * 3,
        [target_rows, decoder_rows],
        0,
        target_rows.size * 4,
    )
    own = [cut[0]] + [passed_along(cut[k], "tgt", k) for k in range(1, blocks)]
    far = [swapped(value, "src", 2) for value in own]
    core = [swapped(value, "src", 1) for value in own]
    cross = [swapped(value, "src", 1) for value in far]

    ordered = source_pos.reshape(2, 2, block).transpose(1, 0, 2).reshape(1, sources)
    tall = heads * queries + block * (groups // 2) + 16
    home = kernel_call(
        functools.partial(payload_kernel, rows),
        shape(tall, sources),
        [own[0], core[0], far[0], cross[0], value_proj, attention, ordered, target_pos[None, :]],
        2 * 4 * sub * depth * groups * head_dim,
        value_proj.size * 2,
    )
    rightward, leftward = [home], [home]
    for step in range(1, blocks):
        up = [(i, i + 1) for i in range(step - 1, blocks - 1)]
        down = [(blocks - 1 - i, blocks - 2 - i) for i in range(step - 1, blocks - 1)]
        rightward.append(lax.ppermute(rightward[-1], "tgt", up))
        leftward.append(lax.ppermute(leftward[-1], "tgt", down))

    reads, direct = kernel_call(
        functools.partial(reads_kernel, rows),
        (
            shape(blocks * targets, heads * head_dim),
            shape(blocks * targets, sources, dtype=F32),
        ),
        [a[k] for k in range(blocks) for a in (own, core, far, cross)] + [out_proj],
        2 * blocks * targets * part * (heads * head_dim + sources),
        out_proj.size * 2,
        [pltpu.VMEM((sources, part), BF16)],
    )

    def edges(flip):
        return kernel_call(
            functools.partial(edges_kernel, heads, queries, flip),
            shape(sources // 2, blocks * targets, dtype=F32),
            [home, *rightward[1:], *leftward[1:], reads, direct, ordered],
            2 * 2 * blocks * targets * sources * heads * head_dim,
            1 << 22,
            [pltpu.VMEM((4,) + home.shape, BF16), pltpu.VMEM((sources, groups * head_dim), BF16)],
        )

    away = swapped(edges(1), "src", 1)
    kept = edges(0)
    back = swapped((kept[:block] + away[:block]).astype(BF16), "src", 2)
    mine = kept[block:] + away[block:] + back.astype(F32)
    parts = [mine[:, k * targets : (k + 1) * targets] for k in range(blocks)]
    landed = [passed_along(parts[k].astype(BF16), "tgt", -k) for k in range(1, blocks)]
    return kernel_call(
        finish_kernel,
        shape(block, targets),
        [tile_pattern, parts[0], *landed],
        4 * block * targets,
        block * targets * 12,
        smem=(0,),
    )


def ring(
    target_rows, target_pos, decoder_rows, source_pos, out_proj, value_proj, attention, tile_pattern
):
    blocks = lax.axis_size("tgt")
    column = lax.axis_index("tgt")
    src_lane = lax.axis_index("src")
    full_targets, full_sources = (
        lax.all_gather(target_rows, "src", axis=0, tiled=True),
        lax.all_gather(decoder_rows, "src", axis=0, tiled=True),
    )
    tgt_dev = full_targets.shape[0]
    src_dev = full_sources.shape[0]
    sub_rows = decoder_rows.shape[0]
    heads_here = out_proj.shape[0]
    head_dim = out_proj.shape[2]
    groups_here = value_proj.shape[0]
    repeat = heads_here // groups_here
    read_sum = jnp.einsum(
        "td,hde->the",
        full_targets,
        lax.all_gather(out_proj, "tgt", axis=1, tiled=True),
        preferred_element_type=jnp.float32,
    )
    head_reads = read_sum.astype(jnp.bfloat16).reshape(tgt_dev, groups_here, repeat, head_dim)
    values = jnp.einsum("sd,gde->sge", full_sources, value_proj, preferred_element_type=jnp.float32)
    values = values.astype(jnp.bfloat16).reshape(src_dev, groups_here * head_dim)
    attn_table = lax.all_gather(attention, "tgt", axis=1, tiled=True)
    target_attn = jnp.take(attn_table, target_pos, axis=1)
    keyed_attn = jnp.transpose(target_attn, (0, 2, 1))

    def edge_tile(payload, block_index):
        decoder_part, value_part = payload
        key_positions = lax.dynamic_slice_in_dim(source_pos, block_index * src_dev, src_dev)
        weights = jnp.take(keyed_attn, key_positions, axis=1).astype(jnp.float32)
        scores = jnp.einsum(
            "sgd,tgrd->grst",
            value_part.reshape(src_dev, groups_here, head_dim),
            head_reads,
            preferred_element_type=jnp.float32,
        )
        scores = scores.reshape(heads_here, src_dev, tgt_dev)
        mixed_term = jnp.sum(weights * scores, axis=0)
        own_positions = lax.dynamic_slice_in_dim(key_positions, src_lane * sub_rows, sub_rows)
        same_place = (own_positions[:, None] == target_pos[None, :]).astype(jnp.float32)
        direct = (
            jnp.einsum("sd,td->st", decoder_part, full_targets, preferred_element_type=jnp.float32)
            * same_place
        )
        own_rows = lax.dynamic_slice_in_dim(mixed_term, src_lane * sub_rows, sub_rows, 0)
        return lax.dynamic_update_slice_in_dim(
            mixed_term, own_rows + direct, src_lane * sub_rows, 0
        )

    def place_tile(partial_value, payload, block_index):
        kept_flag = tile_pattern[block_index, column]
        piece_tile = edge_tile(payload, block_index) * kept_flag.astype(jnp.float32)
        return lax.dynamic_update_slice_in_dim(partial_value, piece_tile, block_index * src_dev, 0)

    own_block = (decoder_rows, values)
    partial_value = jnp.zeros((blocks * src_dev, tgt_dev), jnp.float32)
    partial_value = place_tile(partial_value, own_block, column)

    def cycle_turn(turn_index, state_carry):
        forward_block, backward_block, running = state_carry
        forward_block = passed_along((forward_block[0], forward_block[1]), "tgt", 1)
        backward_block = passed_along((backward_block[0], backward_block[1]), "tgt", -1)
        running = place_tile(running, forward_block, (column - turn_index) % blocks)
        running = place_tile(running, backward_block, (column + turn_index) % blocks)
        return (forward_block, backward_block, running)

    forward_block, backward_block, partial_value = lax.fori_loop(
        1, blocks // 2, cycle_turn, (own_block, own_block, partial_value)
    )
    forward_block = passed_along((forward_block[0], forward_block[1]), "tgt", 1)
    partial_value = place_tile(partial_value, forward_block, (column - blocks // 2) % blocks)
    summed = lax.psum_scatter(partial_value, "src", scatter_dimension=0, tiled=True)
    return summed.astype(jnp.bfloat16)


def shards(*args):
    target_rows, target_pos, decoder_rows, source_pos, out_proj, value_proj, attention, _ = args
    blocks, lanes = lax.axis_size("tgt"), lax.axis_size("src")
    heads, groups = out_proj.shape[0], value_proj.shape[0]
    fits = (
        blocks == 4
        and lanes == 4
        and out_proj.shape[1] % 128 == 0
        and out_proj.shape[2] == 128
        and heads == 2 * groups
        and groups % 2 == 0
        and source_pos.shape[0] == target_pos.shape[0] == attention.shape[2] == 256
        and target_rows.shape[0] % 16 == 0
        and decoder_rows.shape[0] % 16 == 0
        and attention.shape[1] % 16 == 0
    )
    return resident(*args) if fits else ring(*args)


def solution(mesh):
    return jax.shard_map(
        shards,
        mesh=mesh,
        in_specs=(
            P(("grp", "tgt", "src"), None),
            P(("grp", "tgt")),
            P(("grp", "tgt", "src"), None),
            P("grp"),
            P("src", "tgt", None),
            P("src", None, None),
            P(("grp", "src"), "tgt", None),
            P("grp", None),
        ),
        out_specs=P(("grp", "src"), "tgt"),
        check_vma=False,
    )
```

```python
import functools

import jax
import jax.numpy as jnp
from jax import lax
from jax.experimental import pallas as pl
from jax.experimental.pallas import tpu as pltpu
from jax.sharding import PartitionSpec as P


F32 = jnp.float32
BF16 = jnp.bfloat16
VMEM_BYTES = 24 << 20


def passed_along(value, axis, steps):
    count = lax.axis_size(axis)
    pairs = [(source, (source + steps) % count) for source in range(count)]
    return lax.ppermute(value, axis, pairs)


def swapped(value, axis, bit):
    pairs = [(source, source ^ bit) for source in range(lax.axis_size(axis))]
    return lax.ppermute(value, axis, pairs)


def kernel_call(body, outs, args, flops, moved, scratch=(), smem=(), hbm=()):
    return pl.pallas_call(
        body,
        out_shape=outs,
        in_specs=[
            pl.BlockSpec(
                memory_space=pltpu.SMEM if i in smem else pltpu.HBM if i in hbm else pltpu.VMEM
            )
            for i in range(len(args))
        ],
        out_specs=jax.tree.map(lambda _: pl.BlockSpec(memory_space=pltpu.VMEM), outs),
        scratch_shapes=scratch,
        compiler_params=pltpu.CompilerParams(vmem_limit_bytes=VMEM_BYTES),
        cost_estimate=pl.CostEstimate(flops=flops, bytes_accessed=moved, transcendentals=0),
    )(*args)


def aligned(start, size):
    return pl.ds(pl.multiple_of(start, size), size)


def pair_of(ref, first, rows=slice(None)):
    return jnp.concatenate([ref[first, rows, :], ref[first + 1, rows, :]], axis=-1)


def origin_of(z, k):
    return jnp.where(z >= k, z - k, z - k + 4)


def source_row(z, k, block):
    b = origin_of(z, k)
    return (b % 2) * (2 * block) + (b // 2) * block


def cut_kernel(targets, sources, own, first, second, third, done):
    z = lax.axis_index("tgt")
    rows, sub = targets.shape[0], sources.shape[0]
    part = own.shape[1]

    def columns(index):
        return pl.ds(pl.multiple_of(index * part, 128), part)

    moves = [(targets.at[:, columns(z)], own.at[pl.ds(0, rows)])]
    for k, out in enumerate((first, second, third), 1):
        at = columns(jnp.where(z + k >= 4, z + k - 4, z + k))
        moves.append((targets.at[:, at], out.at[pl.ds(0, rows)]))
        moves.append((sources.at[:, at], out.at[pl.ds(rows, sub)]))
    for i in range(4):
        moves.append((sources.at[:, pl.ds(i * part, part)], own.at[pl.ds(rows + i * sub, sub)]))
    copies = [pltpu.make_async_copy(*ends, done.at[i]) for i, ends in enumerate(moves)]
    for copy in copies:
        copy.start()
    for copy in copies:
        copy.wait()


def by_core(positions):
    quarter = positions.shape[1] // 4
    return jnp.concatenate(
        [positions[:, b * quarter : (b + 1) * quarter] for b in (0, 2, 1, 3)], axis=1
    )


def table_kernel(attn, spos, tpos, out):
    heads, queries, keys = attn.shape
    base = heads * queries
    picks = lax.broadcasted_iota(jnp.int32, (keys, spos.shape[1]), 0) == by_core(spos[...])
    picks = picks.astype(F32).astype(BF16)
    table = attn[...].reshape(base, keys)
    out[0:base, :] = jnp.dot(table, picks, preferred_element_type=F32).astype(BF16)
    out[base:, :] = jnp.broadcast_to(
        tpos[...].astype(F32), (out.shape[0] - base, tpos.shape[1])
    ).astype(BF16)


def values_kernel(rows, own, core, far, cross, value, out):
    s = lax.axis_index("src")
    sub = (own.shape[0] - rows) // 4
    part = own.shape[1]
    for pair in range(value.shape[0] // 2):
        total = None
        for i in range(4):
            at = slice(rows + i * sub, rows + (i + 1) * sub)
            left = jnp.concatenate([ref[at, :] for ref in (own, core, far, cross)], axis=0)
            got = jnp.dot(
                left,
                pair_of(value, 2 * pair, slice(i * part, (i + 1) * part)),
                preferred_element_type=F32,
            )
            total = got if total is None else total + got
        width = total.shape[1]
        for j in range(4):
            out[aligned((s ^ j) * sub, sub), pair * width : (pair + 1) * width] = total[
                j * sub : (j + 1) * sub, :
            ].astype(BF16)


def reads_kernel(rows, *refs):
    pieces, weight, reads, direct, dec = refs[:16], refs[16], refs[17], refs[18], refs[19]
    z, s = lax.axis_index("tgt"), lax.axis_index("src")
    sub = pieces[4].shape[0] - rows
    block = 4 * sub
    dec[...] = jnp.zeros_like(dec)
    for k in range(4):
        if k:
            piece = pieces[4 * k][rows:, :]
        else:
            piece = pieces[0][aligned(rows + sub * z, sub), :]
        dec[aligned(source_row(z, k, block) + sub * s, sub), :] = piece
    width = 2 * weight.shape[2]
    group = 4 * rows

    def put(k, target, cols, value):
        for j in range(4):
            target[aligned(k * group + (s ^ j) * rows, rows), cols] = value[
                j * rows : (j + 1) * rows
            ].astype(target.dtype)

    lefts = [
        jnp.concatenate([ref[0:rows, :] for ref in pieces[4 * k : 4 * k + 4]], axis=0)
        for k in range(4)
    ]
    for pair in range(weight.shape[0] // 2):
        right = pair_of(weight, 2 * pair)
        for k in range(4):
            got = jnp.dot(lefts[k], right, preferred_element_type=F32)
            put(k, reads, slice(pair * width, (pair + 1) * width), got)
    for k in range(4):
        got = lax.dot_general(
            lefts[k], dec[...], (((1,), (1,)), ((), ())), preferred_element_type=F32
        )
        put(k, direct, slice(0, direct.shape[1]), got)


def edges_kernel(heads, queries, flip, *refs):
    home, right1, right2, right3, left1, left2, left3 = refs[:7]
    blocks_of_values = refs[7:11]
    reads, direct, spos, out, table, values = refs[11:]
    z, s = lax.axis_index("tgt"), lax.axis_index("src")
    side = (s % 2) ^ flip
    sources = spos.shape[1]
    half = sources // 2
    block = sources // 4
    ordered = by_core(spos[...])
    wide = 2 * (reads.shape[1] // heads)
    dim = wide // 2
    pairs = heads // 2
    table[0] = home[...]
    for k, (near, other) in enumerate(((right1, left3), (right2, left2), (right3, left1)), 1):

        @pl.when(z >= k)
        def _(k=k, near=near):
            table[k] = near[...]

        @pl.when(z < k)
        def _(k=k, other=other):
            table[k] = other[...]

    for k in range(4):
        values[aligned(source_row(z, k, block), block), :] = blocks_of_values[k][...]
    lanes = aligned(side * half, half)
    grid_q = jnp.concatenate(
        [
            lax.broadcasted_iota(jnp.int32, (queries, sources), 0) + origin_of(z, k) * queries
            for k in range(4)
        ],
        axis=0,
    )
    near = ordered[:, :half]
    near = jnp.where(side == 0, near, ordered[:, half:])
    picks = (grid_q[:, :half] == near).astype(F32).astype(BF16)
    blank = jnp.zeros((dim, half), BF16)
    scorers, tables = [], []
    for pair in range(pairs):
        turned = values[lanes, pair * dim : (pair + 1) * dim].astype(F32).T.astype(BF16)
        scorers.append(
            jnp.concatenate(
                [
                    jnp.concatenate([turned, blank], axis=1),
                    jnp.concatenate([blank, turned], axis=1),
                ],
                axis=0,
            )
        )
        tables.append(
            jnp.concatenate(
                [
                    jnp.concatenate(
                        [table[k, h * queries : (h + 1) * queries, lanes] for k in range(4)], axis=0
                    )
                    for h in (2 * pair, 2 * pair + 1)
                ],
                axis=1,
            )
        )
    for k in range(4):
        tpos = table[k, table.shape[1] - 16 : table.shape[1], :].astype(F32)[0:1].astype(jnp.int32)
        hot = (grid_q == tpos).astype(F32).T.astype(BF16)
        here = slice(k * sources, (k + 1) * sources)
        running = None
        for pair in range(pairs):
            weights = jnp.dot(hot, tables[pair], preferred_element_type=F32)
            scores = jnp.dot(
                reads[here, pair * wide : (pair + 1) * wide],
                scorers[pair],
                preferred_element_type=F32,
            )
            term = weights * scores
            running = term if running is None else running + term
        mixed = running[:, :half] + running[:, half:]
        same = jnp.dot(hot, picks, preferred_element_type=F32)
        turned = (mixed + same * direct[here, lanes]).T
        for x in range(2):
            row = jnp.where(s // 2 == x, block, 0)
            out[aligned(row, block), here] = turned[x * block : (x + 1) * block, :]


def finish_kernel(pattern, mine, first, second, third, out):
    kept = pattern[lax.axis_index("src"), lax.axis_index("tgt")].astype(F32)
    total = mine[...]
    for ref in (first, second, third):
        total = total + ref[...].astype(F32)
    out[...] = (total * kept).astype(BF16)


def resident(
    target_rows, target_pos, decoder_rows, source_pos, out_proj, value_proj, attention, tile_pattern
):
    blocks = lax.axis_size("tgt")
    rows, depth = target_rows.shape
    sub = decoder_rows.shape[0]
    part = depth // blocks
    heads, _, head_dim = out_proj.shape
    groups = value_proj.shape[0]
    queries = attention.shape[1]
    sources = source_pos.shape[0]
    targets = target_pos.shape[0]
    block = sources // blocks

    def shape(*dims, dtype=BF16):
        return jax.ShapeDtypeStruct(dims, dtype)

    cut = kernel_call(
        cut_kernel,
        (shape(rows + 4 * sub, part),) + (shape(rows + sub, part),) * 3,
        [target_rows, decoder_rows],
        0,
        target_rows.size * 4,
        [pltpu.SemaphoreType.DMA((11,))],
        hbm=(0, 1),
    )
    own, far, core, cross = [cut[0]], [], [], []
    for k in range(1, blocks):
        own.append(passed_along(cut[k], "tgt", k))
    for k in range(blocks):
        far.append(swapped(own[k], "src", 2))
        core.append(swapped(own[k], "src", 1))
        cross.append(swapped(far[k], "src", 1))

    spots = source_pos[None, :]
    home = kernel_call(
        table_kernel,
        shape(heads * queries + 16, sources),
        [attention, spots, target_pos[None, :]],
        2 * attention.size * sources,
        attention.size * 4,
    )
    rightward, leftward = [home], [home]
    for step in range(1, blocks):
        up = [(i, i + 1) for i in range(step - 1, blocks - 1)]
        down = [(blocks - 1 - i, blocks - 2 - i) for i in range(step - 1, blocks - 1)]
        rightward.append(lax.ppermute(rightward[-1], "tgt", up))
        leftward.append(lax.ppermute(leftward[-1], "tgt", down))
    values = [
        kernel_call(
            functools.partial(values_kernel, rows),
            shape(block, groups * head_dim),
            [own[0], core[0], far[0], cross[0], value_proj],
            2 * block * depth * groups * head_dim,
            value_proj.size * 2,
        )
    ]
    for k in range(1, blocks):
        values.append(passed_along(values[0], "tgt", k))

    reads, direct = kernel_call(
        functools.partial(reads_kernel, rows),
        (
            shape(blocks * targets, heads * head_dim),
            shape(blocks * targets, sources, dtype=F32),
        ),
        [a[k] for k in range(blocks) for a in (own, core, far, cross)] + [out_proj],
        2 * blocks * targets * part * (heads * head_dim + sources),
        out_proj.size * 2,
        [pltpu.VMEM((sources, part), BF16)],
    )

    def edges(flip):
        return kernel_call(
            functools.partial(edges_kernel, heads, queries, flip),
            shape(sources // 2, blocks * targets, dtype=F32),
            [home, *rightward[1:], *leftward[1:], *values, reads, direct, spots],
            2 * 2 * blocks * targets * sources * heads * head_dim,
            1 << 22,
            [pltpu.VMEM((4,) + home.shape, BF16), pltpu.VMEM((sources, groups * head_dim), BF16)],
        )

    away = swapped(edges(1), "src", 1)
    kept = edges(0)
    back = swapped((kept[:block] + away[:block]).astype(BF16), "src", 2)
    mine = kept[block:] + away[block:] + back.astype(F32)
    parts = [mine[:, k * targets : (k + 1) * targets] for k in range(blocks)]
    landed = [passed_along(parts[k].astype(BF16), "tgt", -k) for k in range(1, blocks)]
    return kernel_call(
        finish_kernel,
        shape(block, targets),
        [tile_pattern, parts[0], *landed],
        4 * block * targets,
        block * targets * 12,
        smem=(0,),
    )


def ring(
    target_rows, target_pos, decoder_rows, source_pos, out_proj, value_proj, attention, tile_pattern
):
    blocks = lax.axis_size("tgt")
    column = lax.axis_index("tgt")
    src_lane = lax.axis_index("src")
    full_targets, full_sources = (
        lax.all_gather(target_rows, "src", axis=0, tiled=True),
        lax.all_gather(decoder_rows, "src", axis=0, tiled=True),
    )
    tgt_dev = full_targets.shape[0]
    src_dev = full_sources.shape[0]
    sub_rows = decoder_rows.shape[0]
    heads_here = out_proj.shape[0]
    head_dim = out_proj.shape[2]
    groups_here = value_proj.shape[0]
    repeat = heads_here // groups_here
    read_sum = jnp.einsum(
        "td,hde->the",
        full_targets,
        lax.all_gather(out_proj, "tgt", axis=1, tiled=True),
        preferred_element_type=jnp.float32,
    )
    head_reads = read_sum.astype(jnp.bfloat16).reshape(tgt_dev, groups_here, repeat, head_dim)
    values = jnp.einsum("sd,gde->sge", full_sources, value_proj, preferred_element_type=jnp.float32)
    values = values.astype(jnp.bfloat16).reshape(src_dev, groups_here * head_dim)
    attn_table = lax.all_gather(attention, "tgt", axis=1, tiled=True)
    target_attn = jnp.take(attn_table, target_pos, axis=1)
    keyed_attn = jnp.transpose(target_attn, (0, 2, 1))

    def edge_tile(payload, block_index):
        decoder_part, value_part = payload
        key_positions = lax.dynamic_slice_in_dim(source_pos, block_index * src_dev, src_dev)
        weights = jnp.take(keyed_attn, key_positions, axis=1).astype(jnp.float32)
        scores = jnp.einsum(
            "sgd,tgrd->grst",
            value_part.reshape(src_dev, groups_here, head_dim),
            head_reads,
            preferred_element_type=jnp.float32,
        )
        scores = scores.reshape(heads_here, src_dev, tgt_dev)
        mixed_term = jnp.sum(weights * scores, axis=0)
        own_positions = lax.dynamic_slice_in_dim(key_positions, src_lane * sub_rows, sub_rows)
        same_place = (own_positions[:, None] == target_pos[None, :]).astype(jnp.float32)
        direct = (
            jnp.einsum("sd,td->st", decoder_part, full_targets, preferred_element_type=jnp.float32)
            * same_place
        )
        own_rows = lax.dynamic_slice_in_dim(mixed_term, src_lane * sub_rows, sub_rows, 0)
        return lax.dynamic_update_slice_in_dim(
            mixed_term, own_rows + direct, src_lane * sub_rows, 0
        )

    def place_tile(partial_value, payload, block_index):
        kept_flag = tile_pattern[block_index, column]
        piece_tile = edge_tile(payload, block_index) * kept_flag.astype(jnp.float32)
        return lax.dynamic_update_slice_in_dim(partial_value, piece_tile, block_index * src_dev, 0)

    own_block = (decoder_rows, values)
    partial_value = jnp.zeros((blocks * src_dev, tgt_dev), jnp.float32)
    partial_value = place_tile(partial_value, own_block, column)

    def cycle_turn(turn_index, state_carry):
        forward_block, backward_block, running = state_carry
        forward_block = passed_along((forward_block[0], forward_block[1]), "tgt", 1)
        backward_block = passed_along((backward_block[0], backward_block[1]), "tgt", -1)
        running = place_tile(running, forward_block, (column - turn_index) % blocks)
        running = place_tile(running, backward_block, (column + turn_index) % blocks)
        return (forward_block, backward_block, running)

    forward_block, _, partial_value = lax.fori_loop(
        1, blocks // 2, cycle_turn, (own_block, own_block, partial_value)
    )
    forward_block = passed_along((forward_block[0], forward_block[1]), "tgt", 1)
    partial_value = place_tile(partial_value, forward_block, (column - blocks // 2) % blocks)
    summed = lax.psum_scatter(partial_value, "src", scatter_dimension=0, tiled=True)
    return summed.astype(jnp.bfloat16)


def shards(*args):
    target_rows, target_pos, decoder_rows, source_pos, out_proj, value_proj, attention, _ = args
    blocks, lanes = lax.axis_size("tgt"), lax.axis_size("src")
    heads, groups = out_proj.shape[0], value_proj.shape[0]
    fits = (
        blocks == 4
        and lanes == 4
        and out_proj.shape[1] % 128 == 0
        and out_proj.shape[2] == 128
        and heads == 2 * groups
        and groups % 2 == 0
        and source_pos.shape[0] == target_pos.shape[0] == attention.shape[2] == 256
        and target_rows.shape[0] % 16 == 0
        and decoder_rows.shape[0] % 16 == 0
        and attention.shape[1] % 16 == 0
    )
    if not fits:
        return ring(*args)
    return resident(*args)


def solution(mesh):
    return jax.shard_map(
        shards,
        mesh=mesh,
        in_specs=(
            P(("grp", "tgt", "src"), None),
            P(("grp", "tgt")),
            P(("grp", "tgt", "src"), None),
            P("grp"),
            P("src", "tgt", None),
            P("src", None, None),
            P(("grp", "src"), "tgt", None),
            P("grp", None),
        ),
        out_specs=P(("grp", "src"), "tgt"),
        check_vma=False,
    )
```

```python
import functools

import jax
import jax.numpy as jnp
from jax import lax
from jax.experimental import pallas as pl
from jax.experimental.pallas import tpu as pltpu
from jax.sharding import PartitionSpec as P


F32 = jnp.float32
BF16 = jnp.bfloat16
VMEM_BYTES = 24 << 20


def passed_along(value, axis, steps):
    count = lax.axis_size(axis)
    pairs = [(source, (source + steps) % count) for source in range(count)]
    return lax.ppermute(value, axis, pairs)


def swapped(value, axis, bit):
    pairs = [(source, source ^ bit) for source in range(lax.axis_size(axis))]
    return lax.ppermute(value, axis, pairs)


def kernel_call(body, outs, args, flops, moved, scratch=(), smem=(), hbm=()):
    return pl.pallas_call(
        body,
        out_shape=outs,
        in_specs=[
            pl.BlockSpec(
                memory_space=pltpu.SMEM if i in smem else pltpu.HBM if i in hbm else pltpu.VMEM
            )
            for i in range(len(args))
        ],
        out_specs=jax.tree.map(lambda _: pl.BlockSpec(memory_space=pltpu.VMEM), outs),
        scratch_shapes=scratch,
        compiler_params=pltpu.CompilerParams(vmem_limit_bytes=VMEM_BYTES),
        cost_estimate=pl.CostEstimate(flops=flops, bytes_accessed=moved, transcendentals=0),
    )(
        *[
            pltpu.with_memory_space_constraint(arg, pltpu.HBM) if i in hbm else arg
            for i, arg in enumerate(args)
        ]
    )


def aligned(start, size):
    return pl.ds(pl.multiple_of(start, size), size)


def pair_of(ref, first, rows=slice(None)):
    return jnp.concatenate([ref[first, rows, :], ref[first + 1, rows, :]], axis=-1)


def origin_of(z, k):
    return jnp.where(z >= k, z - k, z - k + 4)


def source_row(z, k, block):
    b = origin_of(z, k)
    return (b % 2) * (2 * block) + (b // 2) * block


def by_core(positions):
    quarter = positions.shape[1] // 4
    return jnp.concatenate(
        [positions[:, b * quarter : (b + 1) * quarter] for b in (0, 2, 1, 3)], axis=1
    )


def front_kernel(targets, sources, attn, spos, tpos, own, first, second, third, table, held, spots, done):
    z = lax.axis_index("tgt")
    rows, sub = targets.shape[0], sources.shape[0]
    part = own.shape[1]
    heads, queries, keys = attn.shape
    base = heads * queries

    def columns(index):
        return pl.ds(pl.multiple_of(index * part, 128), part)

    moves = [(attn, held), (spos, spots.at[0]), (tpos, spots.at[1])]
    for k, out in enumerate((first, second, third), 1):
        at = columns(jnp.where(z + k >= 4, z + k - 4, z + k))
        moves.append((targets.at[:, at], out.at[pl.ds(0, rows)]))
        moves.append((sources.at[:, at], out.at[pl.ds(rows, sub)]))
    moves.append((targets.at[:, columns(z)], own.at[pl.ds(0, rows)]))
    for i in range(4):
        moves.append((sources.at[:, pl.ds(i * part, part)], own.at[pl.ds(rows + i * sub, sub)]))
    copies = [pltpu.make_async_copy(*ends, done.at[i]) for i, ends in enumerate(moves)]
    for copy in copies:
        copy.start()
    for copy in copies[:3]:
        copy.wait()
    picks = lax.broadcasted_iota(jnp.int32, (keys, spos.shape[1]), 0) == by_core(spots[0])
    picks = picks.astype(F32).astype(BF16)
    table[0:base, :] = jnp.dot(
        held[...].reshape(base, keys), picks, preferred_element_type=F32
    ).astype(BF16)
    table[base:, :] = jnp.broadcast_to(
        spots[1].astype(F32), (table.shape[0] - base, tpos.shape[1])
    ).astype(BF16)
    for copy in copies[3:]:
        copy.wait()


def values_kernel(rows, own, core, far, cross, value, out, held, done):
    s = lax.axis_index("src")
    sub = (own.shape[0] - rows) // 4
    part = own.shape[1]
    pairs = value.shape[0] // 2
    copies = [
        pltpu.make_async_copy(
            value.at[:, pl.ds(i * part, part), :], held.at[:, pl.ds(i * part, part), :], done.at[i]
        )
        for i in range(4)
    ]
    for copy in copies:
        copy.start()
    totals = [None] * pairs
    for i in range(4):
        copies[i].wait()
        at = slice(rows + i * sub, rows + (i + 1) * sub)
        left = jnp.concatenate([ref[at, :] for ref in (own, core, far, cross)], axis=0)
        for pair in range(pairs):
            got = jnp.dot(
                left,
                pair_of(held, 2 * pair, slice(i * part, (i + 1) * part)),
                preferred_element_type=F32,
            )
            totals[pair] = got if i == 0 else totals[pair] + got
    for pair, total in enumerate(totals):
        width = total.shape[1]
        for j in range(4):
            out[aligned((s ^ j) * sub, sub), pair * width : (pair + 1) * width] = total[
                j * sub : (j + 1) * sub, :
            ].astype(BF16)


def reads_kernel(rows, *refs):
    pieces, weight, reads, direct, dec = refs[:16], refs[16], refs[17], refs[18], refs[19]
    z, s = lax.axis_index("tgt"), lax.axis_index("src")
    sub = pieces[4].shape[0] - rows
    block = 4 * sub
    dec[...] = jnp.zeros_like(dec)
    for k in range(4):
        if k:
            piece = pieces[4 * k][rows:, :]
        else:
            piece = pieces[0][aligned(rows + sub * z, sub), :]
        dec[aligned(source_row(z, k, block) + sub * s, sub), :] = piece
    width = 2 * weight.shape[2]
    group = 4 * rows

    def put(k, target, cols, value):
        for j in range(4):
            target[aligned(k * group + (s ^ j) * rows, rows), cols] = value[
                j * rows : (j + 1) * rows
            ].astype(target.dtype)

    lefts = [
        jnp.concatenate([ref[0:rows, :] for ref in pieces[4 * k : 4 * k + 4]], axis=0)
        for k in range(4)
    ]
    for pair in range(weight.shape[0] // 2):
        right = pair_of(weight, 2 * pair)
        for k in range(4):
            got = jnp.dot(lefts[k], right, preferred_element_type=F32)
            put(k, reads, slice(pair * width, (pair + 1) * width), got)
    for k in range(4):
        got = lax.dot_general(
            lefts[k], dec[...], (((1,), (1,)), ((), ())), preferred_element_type=F32
        )
        put(k, direct, slice(0, direct.shape[1]), got)


def edges_kernel(heads, queries, flip, *refs):
    home, right1, right2, right3, left1, left2, left3 = refs[:7]
    blocks_of_values = refs[7:11]
    reads, direct, spos, pattern, out, table, values = refs[11:]
    z, s = lax.axis_index("tgt"), lax.axis_index("src")
    side = (s % 2) ^ flip
    sources = spos.shape[1]
    half = sources // 2
    block = sources // 4
    ordered = by_core(spos[...])
    wide = 2 * (reads.shape[1] // heads)
    dim = wide // 2
    pairs = heads // 2
    table[0] = home[...]
    for k, (near, other) in enumerate(((right1, left3), (right2, left2), (right3, left1)), 1):

        @pl.when(z >= k)
        def _(k=k, near=near):
            table[k] = near[...]

        @pl.when(z < k)
        def _(k=k, other=other):
            table[k] = other[...]

    for k in range(4):
        values[aligned(source_row(z, k, block), block), :] = blocks_of_values[k][...]
    lanes = aligned(side * half, half)
    grid_q = jnp.concatenate(
        [
            lax.broadcasted_iota(jnp.int32, (queries, sources), 0) + origin_of(z, k) * queries
            for k in range(4)
        ],
        axis=0,
    )
    near = ordered[:, :half]
    near = jnp.where(side == 0, near, ordered[:, half:])
    picks = (grid_q[:, :half] == near).astype(F32).astype(BF16)
    blank = jnp.zeros((dim, half), BF16)
    scorers, tables = [], []
    for pair in range(pairs):
        turned = values[lanes, pair * dim : (pair + 1) * dim].astype(F32).T.astype(BF16)
        scorers.append(
            jnp.concatenate(
                [
                    jnp.concatenate([turned, blank], axis=1),
                    jnp.concatenate([blank, turned], axis=1),
                ],
                axis=0,
            )
        )
        tables.append(
            jnp.concatenate(
                [
                    jnp.concatenate(
                        [table[k, h * queries : (h + 1) * queries, lanes] for k in range(4)], axis=0
                    )
                    for h in (2 * pair, 2 * pair + 1)
                ],
                axis=1,
            )
        )
    for k in range(4):
        tpos = table[k, table.shape[1] - 16 : table.shape[1], :].astype(F32)[0:1].astype(jnp.int32)
        hot = (grid_q == tpos).astype(F32).T.astype(BF16)
        here = slice(k * sources, (k + 1) * sources)
        running = None
        for pair in range(pairs):
            weights = jnp.dot(hot, tables[pair], preferred_element_type=F32)
            scores = jnp.dot(
                reads[here, pair * wide : (pair + 1) * wide],
                scorers[pair],
                preferred_element_type=F32,
            )
            term = weights * scores
            running = term if running is None else running + term
        mixed = running[:, :half] + running[:, half:]
        same = jnp.dot(hot, picks, preferred_element_type=F32)
        turned = (mixed + same * direct[here, lanes]).T
        for x in range(2):
            row = jnp.where(s // 2 == x, block, 0)
            kept = pattern[2 * x + side, origin_of(z, k)].astype(F32)
            out[aligned(row, block), here] = turned[x * block : (x + 1) * block, :] * kept


def resident(
    target_rows, target_pos, decoder_rows, source_pos, out_proj, value_proj, attention, tile_pattern
):
    blocks = lax.axis_size("tgt")
    rows, depth = target_rows.shape
    sub = decoder_rows.shape[0]
    part = depth // blocks
    heads, _, head_dim = out_proj.shape
    groups = value_proj.shape[0]
    queries = attention.shape[1]
    sources = source_pos.shape[0]
    targets = target_pos.shape[0]
    block = sources // blocks

    def shape(*dims, dtype=BF16):
        return jax.ShapeDtypeStruct(dims, dtype)

    spots = source_pos[None, :]
    cut = kernel_call(
        front_kernel,
        (shape(rows + 4 * sub, part),)
        + (shape(rows + sub, part),) * 3
        + (shape(heads * queries + 16, sources),),
        [target_rows, decoder_rows, attention, spots, target_pos[None, :]],
        2 * attention.size * sources,
        target_rows.size * 4,
        [
            pltpu.VMEM(attention.shape, BF16),
            pltpu.VMEM((2, 1, sources), jnp.int32),
            pltpu.SemaphoreType.DMA((14,)),
        ],
        hbm=(0, 1, 2, 3, 4),
    )
    own, far, core, cross = [cut[0]], [], [], []
    for k in range(1, blocks):
        own.append(passed_along(cut[k], "tgt", k))
    for k in range(blocks):
        far.append(swapped(own[k], "src", 2))
        core.append(swapped(own[k], "src", 1))
        cross.append(swapped(far[k], "src", 1))

    home = cut[4]
    rightward, leftward = [home], [home]
    for step in range(1, blocks):
        up = [(i, i + 1) for i in range(step - 1, blocks - 1)]
        down = [(blocks - 1 - i, blocks - 2 - i) for i in range(step - 1, blocks - 1)]
        rightward.append(lax.ppermute(rightward[-1], "tgt", up))
        leftward.append(lax.ppermute(leftward[-1], "tgt", down))
    values = [
        kernel_call(
            functools.partial(values_kernel, rows),
            shape(block, groups * head_dim),
            [own[0], core[0], far[0], cross[0], value_proj],
            2 * block * depth * groups * head_dim,
            value_proj.size * 2,
            [pltpu.VMEM(value_proj.shape, BF16), pltpu.SemaphoreType.DMA((4,))],
            hbm=(4,),
        )
    ]
    for k in range(1, blocks):
        values.append(passed_along(values[0], "tgt", k))

    reads, direct = kernel_call(
        functools.partial(reads_kernel, rows),
        (
            shape(blocks * targets, heads * head_dim),
            shape(blocks * targets, sources, dtype=F32),
        ),
        [a[k] for k in range(blocks) for a in (own, core, far, cross)] + [out_proj],
        2 * blocks * targets * part * (heads * head_dim + sources),
        out_proj.size * 2,
        [pltpu.VMEM((sources, part), BF16)],
    )

    def edges(flip):
        return kernel_call(
            functools.partial(edges_kernel, heads, queries, flip),
            shape(sources // 2, blocks * targets, dtype=F32),
            [home, *rightward[1:], *leftward[1:], *values, reads, direct, spots, tile_pattern],
            2 * 2 * blocks * targets * sources * heads * head_dim,
            1 << 22,
            [pltpu.VMEM((4,) + home.shape, BF16), pltpu.VMEM((sources, groups * head_dim), BF16)],
            smem=(14,),
        )

    away = swapped(edges(1), "src", 1)
    kept = edges(0)
    back = swapped((kept[:block] + away[:block]).astype(BF16), "src", 2)
    mine = kept[block:] + away[block:] + back.astype(F32)
    parts = [mine[:, k * targets : (k + 1) * targets] for k in range(blocks)]
    landed = [passed_along(parts[k].astype(BF16), "tgt", -k) for k in range(1, blocks)]
    result = parts[0]
    for value in landed:
        result = result + value.astype(F32)
    return result.astype(BF16)


def ring(
    target_rows, target_pos, decoder_rows, source_pos, out_proj, value_proj, attention, tile_pattern
):
    blocks = lax.axis_size("tgt")
    column = lax.axis_index("tgt")
    src_lane = lax.axis_index("src")
    full_targets, full_sources = (
        lax.all_gather(target_rows, "src", axis=0, tiled=True),
        lax.all_gather(decoder_rows, "src", axis=0, tiled=True),
    )
    tgt_dev = full_targets.shape[0]
    src_dev = full_sources.shape[0]
    sub_rows = decoder_rows.shape[0]
    heads_here = out_proj.shape[0]
    head_dim = out_proj.shape[2]
    groups_here = value_proj.shape[0]
    repeat = heads_here // groups_here
    read_sum = jnp.einsum(
        "td,hde->the",
        full_targets,
        lax.all_gather(out_proj, "tgt", axis=1, tiled=True),
        preferred_element_type=jnp.float32,
    )
    head_reads = read_sum.astype(jnp.bfloat16).reshape(tgt_dev, groups_here, repeat, head_dim)
    values = jnp.einsum("sd,gde->sge", full_sources, value_proj, preferred_element_type=jnp.float32)
    values = values.astype(jnp.bfloat16).reshape(src_dev, groups_here * head_dim)
    attn_table = lax.all_gather(attention, "tgt", axis=1, tiled=True)
    target_attn = jnp.take(attn_table, target_pos, axis=1)
    keyed_attn = jnp.transpose(target_attn, (0, 2, 1))

    def edge_tile(payload, block_index):
        decoder_part, value_part = payload
        key_positions = lax.dynamic_slice_in_dim(source_pos, block_index * src_dev, src_dev)
        weights = jnp.take(keyed_attn, key_positions, axis=1).astype(jnp.float32)
        scores = jnp.einsum(
            "sgd,tgrd->grst",
            value_part.reshape(src_dev, groups_here, head_dim),
            head_reads,
            preferred_element_type=jnp.float32,
        )
        scores = scores.reshape(heads_here, src_dev, tgt_dev)
        mixed_term = jnp.sum(weights * scores, axis=0)
        own_positions = lax.dynamic_slice_in_dim(key_positions, src_lane * sub_rows, sub_rows)
        same_place = (own_positions[:, None] == target_pos[None, :]).astype(jnp.float32)
        direct = (
            jnp.einsum("sd,td->st", decoder_part, full_targets, preferred_element_type=jnp.float32)
            * same_place
        )
        own_rows = lax.dynamic_slice_in_dim(mixed_term, src_lane * sub_rows, sub_rows, 0)
        return lax.dynamic_update_slice_in_dim(
            mixed_term, own_rows + direct, src_lane * sub_rows, 0
        )

    def place_tile(partial_value, payload, block_index):
        kept_flag = tile_pattern[block_index, column]
        piece_tile = edge_tile(payload, block_index) * kept_flag.astype(jnp.float32)
        return lax.dynamic_update_slice_in_dim(partial_value, piece_tile, block_index * src_dev, 0)

    own_block = (decoder_rows, values)
    partial_value = jnp.zeros((blocks * src_dev, tgt_dev), jnp.float32)
    partial_value = place_tile(partial_value, own_block, column)

    def cycle_turn(turn_index, state_carry):
        forward_block, backward_block, running = state_carry
        forward_block = passed_along((forward_block[0], forward_block[1]), "tgt", 1)
        backward_block = passed_along((backward_block[0], backward_block[1]), "tgt", -1)
        running = place_tile(running, forward_block, (column - turn_index) % blocks)
        running = place_tile(running, backward_block, (column + turn_index) % blocks)
        return (forward_block, backward_block, running)

    forward_block, _, partial_value = lax.fori_loop(
        1, blocks // 2, cycle_turn, (own_block, own_block, partial_value)
    )
    forward_block = passed_along((forward_block[0], forward_block[1]), "tgt", 1)
    partial_value = place_tile(partial_value, forward_block, (column - blocks // 2) % blocks)
    summed = lax.psum_scatter(partial_value, "src", scatter_dimension=0, tiled=True)
    return summed.astype(jnp.bfloat16)


def shards(*args):
    target_rows, target_pos, decoder_rows, source_pos, out_proj, value_proj, attention, _ = args
    blocks, lanes = lax.axis_size("tgt"), lax.axis_size("src")
    heads, groups = out_proj.shape[0], value_proj.shape[0]
    fits = (
        blocks == 4
        and lanes == 4
        and out_proj.shape[1] % 128 == 0
        and out_proj.shape[2] == 128
        and heads == 2 * groups
        and groups % 2 == 0
        and source_pos.shape[0] == target_pos.shape[0] == attention.shape[2] == 256
        and target_rows.shape[0] % 16 == 0
        and decoder_rows.shape[0] % 16 == 0
        and attention.shape[1] % 16 == 0
    )
    if not fits:
        return ring(*args)
    return resident(*args)


def solution(mesh):
    return jax.shard_map(
        shards,
        mesh=mesh,
        in_specs=(
            P(("grp", "tgt", "src"), None),
            P(("grp", "tgt")),
            P(("grp", "tgt", "src"), None),
            P("grp"),
            P("src", "tgt", None),
            P("src", None, None),
            P(("grp", "src"), "tgt", None),
            P("grp", None),
        ),
        out_specs=P(("grp", "src"), "tgt"),
        check_vma=False,
    )
```

```python
import functools

import jax
import jax.numpy as jnp
from jax import lax
from jax.experimental import pallas as pl
from jax.experimental.pallas import tpu as pltpu
from jax.sharding import PartitionSpec as P


F32 = jnp.float32
BF16 = jnp.bfloat16
VMEM_BYTES = 24 << 20


def passed_along(value, axis, steps):
    count = lax.axis_size(axis)
    pairs = [(source, (source + steps) % count) for source in range(count)]
    return lax.ppermute(value, axis, pairs)


def swapped(value, axis, bit):
    pairs = [(source, source ^ bit) for source in range(lax.axis_size(axis))]
    return lax.ppermute(value, axis, pairs)


def kernel_call(body, outs, args, flops, moved, scratch=(), smem=(), hbm=()):
    return pl.pallas_call(
        body,
        out_shape=outs,
        in_specs=[
            pl.BlockSpec(
                memory_space=pltpu.SMEM if i in smem else pltpu.HBM if i in hbm else pltpu.VMEM
            )
            for i in range(len(args))
        ],
        out_specs=jax.tree.map(lambda _: pl.BlockSpec(memory_space=pltpu.VMEM), outs),
        scratch_shapes=scratch,
        compiler_params=pltpu.CompilerParams(vmem_limit_bytes=VMEM_BYTES),
        cost_estimate=pl.CostEstimate(flops=flops, bytes_accessed=moved, transcendentals=0),
    )(
        *[
            pltpu.with_memory_space_constraint(arg, pltpu.HBM) if i in hbm else arg
            for i, arg in enumerate(args)
        ]
    )


def aligned(start, size):
    return pl.ds(pl.multiple_of(start, size), size)


def pair_of(ref, first, rows=slice(None)):
    return jnp.concatenate([ref[first, rows, :], ref[first + 1, rows, :]], axis=-1)


def origin_of(z, k):
    return jnp.where(z >= k, z - k, z - k + 4)


def source_row(z, k, block):
    b = origin_of(z, k)
    return (b % 2) * (2 * block) + (b // 2) * block


def by_core(positions):
    quarter = positions.shape[1] // 4
    return jnp.concatenate(
        [positions[:, b * quarter : (b + 1) * quarter] for b in (0, 2, 1, 3)], axis=1
    )


def front_kernel(
    targets, sources, attn, spos, tpos, pattern, own, first, second, third, table, kept, held, spots, flags, done
):
    z = lax.axis_index("tgt")
    rows, sub = targets.shape[0], sources.shape[0]
    part = own.shape[1]
    heads, queries, keys = attn.shape
    base = heads * queries

    def columns(index):
        return pl.ds(pl.multiple_of(index * part, 128), part)

    moves = [(attn, held), (spos, spots.at[0]), (tpos, spots.at[1]), (pattern, flags)]
    for k, out in enumerate((first, second, third), 1):
        at = columns(jnp.where(z + k >= 4, z + k - 4, z + k))
        moves.append((targets.at[:, at], out.at[pl.ds(0, rows)]))
        moves.append((sources.at[:, at], out.at[pl.ds(rows, sub)]))
    moves.append((targets.at[:, columns(z)], own.at[pl.ds(0, rows)]))
    for i in range(4):
        moves.append((sources.at[:, pl.ds(i * part, part)], own.at[pl.ds(rows + i * sub, sub)]))
    copies = [pltpu.make_async_copy(*ends, done.at[i]) for i, ends in enumerate(moves)]
    for copy in copies:
        copy.start()
    for copy in copies[:4]:
        copy.wait()
    picks = lax.broadcasted_iota(jnp.int32, (keys, spos.shape[1]), 0) == by_core(spots[0])
    picks = picks.astype(F32).astype(BF16)
    table[0:base, :] = jnp.dot(
        held[...].reshape(base, keys), picks, preferred_element_type=F32
    ).astype(BF16)
    table[base:, :] = jnp.broadcast_to(
        spots[1].astype(F32), (table.shape[0] - base, tpos.shape[1])
    ).astype(BF16)
    across = lax.broadcasted_iota(jnp.int32, pattern.shape, 0) == lax.axis_index("src")
    down = lax.broadcasted_iota(jnp.int32, pattern.shape, 1) == z
    flag = jnp.where(across & down, flags[...], 0).astype(F32)
    kept[...] = jnp.broadcast_to(jnp.sum(flag, keepdims=True), kept.shape)
    for copy in copies[4:]:
        copy.wait()


def values_kernel(rows, own, core, far, cross, value, out, held, done):
    s = lax.axis_index("src")
    sub = (own.shape[0] - rows) // 4
    part = own.shape[1]
    pairs = value.shape[0] // 2
    copies = [
        pltpu.make_async_copy(
            value.at[:, pl.ds(i * part, part), :], held.at[:, pl.ds(i * part, part), :], done.at[i]
        )
        for i in range(4)
    ]
    for copy in copies:
        copy.start()
    totals = [None] * pairs
    for i in range(4):
        copies[i].wait()
        at = slice(rows + i * sub, rows + (i + 1) * sub)
        left = jnp.concatenate([ref[at, :] for ref in (own, core, far, cross)], axis=0)
        for pair in range(pairs):
            got = jnp.dot(
                left,
                pair_of(held, 2 * pair, slice(i * part, (i + 1) * part)),
                preferred_element_type=F32,
            )
            totals[pair] = got if i == 0 else totals[pair] + got
    for pair, total in enumerate(totals):
        width = total.shape[1]
        for j in range(4):
            out[aligned((s ^ j) * sub, sub), pair * width : (pair + 1) * width] = total[
                j * sub : (j + 1) * sub, :
            ].astype(BF16)


def reads_kernel(rows, *refs):
    pieces, weight, reads, direct, dec = refs[:16], refs[16], refs[17], refs[18], refs[19]
    z, s = lax.axis_index("tgt"), lax.axis_index("src")
    sub = pieces[4].shape[0] - rows
    block = 4 * sub
    dec[...] = jnp.zeros_like(dec)
    for k in range(4):
        if k:
            piece = pieces[4 * k][rows:, :]
        else:
            piece = pieces[0][aligned(rows + sub * z, sub), :]
        dec[aligned(source_row(z, k, block) + sub * s, sub), :] = piece
    width = 2 * weight.shape[2]
    group = 4 * rows

    def put(k, target, cols, value):
        for j in range(4):
            target[aligned(k * group + (s ^ j) * rows, rows), cols] = value[
                j * rows : (j + 1) * rows
            ].astype(target.dtype)

    lefts = [
        jnp.concatenate([ref[0:rows, :] for ref in pieces[4 * k : 4 * k + 4]], axis=0)
        for k in range(4)
    ]
    for pair in range(weight.shape[0] // 2):
        right = pair_of(weight, 2 * pair)
        for k in range(4):
            got = jnp.dot(lefts[k], right, preferred_element_type=F32)
            put(k, reads, slice(pair * width, (pair + 1) * width), got)
    for k in range(4):
        got = lax.dot_general(
            lefts[k], dec[...], (((1,), (1,)), ((), ())), preferred_element_type=F32
        )
        put(k, direct, slice(0, direct.shape[1]), got)


def edges_kernel(heads, queries, flip, *refs):
    home, right1, right2, right3, left1, left2, left3 = refs[:7]
    blocks_of_values = refs[7:11]
    reads, direct, spos, out, table, values = refs[11:]
    z, s = lax.axis_index("tgt"), lax.axis_index("src")
    side = (s % 2) ^ flip
    sources = spos.shape[1]
    half = sources // 2
    block = sources // 4
    ordered = by_core(spos[...])
    wide = 2 * (reads.shape[1] // heads)
    dim = wide // 2
    pairs = heads // 2
    table[0] = home[...]
    for k, (near, other) in enumerate(((right1, left3), (right2, left2), (right3, left1)), 1):

        @pl.when(z >= k)
        def _(k=k, near=near):
            table[k] = near[...]

        @pl.when(z < k)
        def _(k=k, other=other):
            table[k] = other[...]

    for k in range(4):
        values[aligned(source_row(z, k, block), block), :] = blocks_of_values[k][...]
    lanes = aligned(side * half, half)
    grid_q = jnp.concatenate(
        [
            lax.broadcasted_iota(jnp.int32, (queries, sources), 0) + origin_of(z, k) * queries
            for k in range(4)
        ],
        axis=0,
    )
    near = ordered[:, :half]
    near = jnp.where(side == 0, near, ordered[:, half:])
    picks = (grid_q[:, :half] == near).astype(F32).astype(BF16)
    blank = jnp.zeros((dim, half), BF16)
    scorers, tables = [], []
    for pair in range(pairs):
        turned = values[lanes, pair * dim : (pair + 1) * dim].astype(F32).T.astype(BF16)
        scorers.append(
            jnp.concatenate(
                [
                    jnp.concatenate([turned, blank], axis=1),
                    jnp.concatenate([blank, turned], axis=1),
                ],
                axis=0,
            )
        )
        tables.append(
            jnp.concatenate(
                [
                    jnp.concatenate(
                        [table[k, h * queries : (h + 1) * queries, lanes] for k in range(4)], axis=0
                    )
                    for h in (2 * pair, 2 * pair + 1)
                ],
                axis=1,
            )
        )
    for k in range(4):
        tpos = table[k, table.shape[1] - 16 : table.shape[1], :].astype(F32)[0:1].astype(jnp.int32)
        hot = (grid_q == tpos).astype(F32).T.astype(BF16)
        here = slice(k * sources, (k + 1) * sources)
        running = None
        for pair in range(pairs):
            weights = jnp.dot(hot, tables[pair], preferred_element_type=F32)
            scores = jnp.dot(
                reads[here, pair * wide : (pair + 1) * wide],
                scorers[pair],
                preferred_element_type=F32,
            )
            term = weights * scores
            running = term if running is None else running + term
        mixed = running[:, :half] + running[:, half:]
        same = jnp.dot(hot, picks, preferred_element_type=F32)
        turned = (mixed + same * direct[here, lanes]).T
        for x in range(2):
            row = jnp.where(s // 2 == x, block, 0)
            out[aligned(row, block), here] = turned[x * block : (x + 1) * block, :]


def resident(
    target_rows, target_pos, decoder_rows, source_pos, out_proj, value_proj, attention, tile_pattern
):
    blocks = lax.axis_size("tgt")
    rows, depth = target_rows.shape
    sub = decoder_rows.shape[0]
    part = depth // blocks
    heads, _, head_dim = out_proj.shape
    groups = value_proj.shape[0]
    queries = attention.shape[1]
    sources = source_pos.shape[0]
    targets = target_pos.shape[0]
    block = sources // blocks

    def shape(*dims, dtype=BF16):
        return jax.ShapeDtypeStruct(dims, dtype)

    spots = source_pos[None, :]
    cut = kernel_call(
        front_kernel,
        (shape(rows + 4 * sub, part),)
        + (shape(rows + sub, part),) * 3
        + (shape(heads * queries + 16, sources), shape(1, targets, dtype=F32)),
        [target_rows, decoder_rows, attention, spots, target_pos[None, :], tile_pattern],
        2 * attention.size * sources,
        target_rows.size * 4,
        [
            pltpu.VMEM(attention.shape, BF16),
            pltpu.VMEM((2, 1, sources), jnp.int32),
            pltpu.VMEM(tile_pattern.shape, jnp.int32),
            pltpu.SemaphoreType.DMA((15,)),
        ],
        hbm=(0, 1, 2, 3, 4, 5),
    )
    own, far, core, cross = [cut[0]], [], [], []
    for k in range(1, blocks):
        own.append(passed_along(cut[k], "tgt", k))
    for k in range(blocks):
        far.append(swapped(own[k], "src", 2))
        core.append(swapped(own[k], "src", 1))
        cross.append(swapped(far[k], "src", 1))

    home = cut[4]
    rightward, leftward = [home], [home]
    for step in range(1, blocks):
        up = [(i, i + 1) for i in range(step - 1, blocks - 1)]
        down = [(blocks - 1 - i, blocks - 2 - i) for i in range(step - 1, blocks - 1)]
        rightward.append(lax.ppermute(rightward[-1], "tgt", up))
        leftward.append(lax.ppermute(leftward[-1], "tgt", down))
    values = [
        kernel_call(
            functools.partial(values_kernel, rows),
            shape(block, groups * head_dim),
            [own[0], core[0], far[0], cross[0], value_proj],
            2 * block * depth * groups * head_dim,
            value_proj.size * 2,
            [pltpu.VMEM(value_proj.shape, BF16), pltpu.SemaphoreType.DMA((4,))],
            hbm=(4,),
        )
    ]
    for k in range(1, blocks):
        values.append(passed_along(values[0], "tgt", k))

    reads, direct = kernel_call(
        functools.partial(reads_kernel, rows),
        (
            shape(blocks * targets, heads * head_dim),
            shape(blocks * targets, sources, dtype=F32),
        ),
        [a[k] for k in range(blocks) for a in (own, core, far, cross)] + [out_proj],
        2 * blocks * targets * part * (heads * head_dim + sources),
        out_proj.size * 2,
        [pltpu.VMEM((sources, part), BF16)],
    )

    def edges(flip):
        return kernel_call(
            functools.partial(edges_kernel, heads, queries, flip),
            shape(sources // 2, blocks * targets, dtype=F32),
            [home, *rightward[1:], *leftward[1:], *values, reads, direct, spots],
            2 * 2 * blocks * targets * sources * heads * head_dim,
            1 << 22,
            [pltpu.VMEM((4,) + home.shape, BF16), pltpu.VMEM((sources, groups * head_dim), BF16)],
        )

    away = swapped(edges(1), "src", 1)
    kept = edges(0)
    back = swapped((kept[:block] + away[:block]).astype(BF16), "src", 2)
    mine = kept[block:] + away[block:] + back.astype(F32)
    parts = [mine[:, k * targets : (k + 1) * targets] for k in range(blocks)]
    landed = [passed_along(parts[k].astype(BF16), "tgt", -k) for k in range(1, blocks)]
    result = parts[0]
    for value in landed:
        result = result + value.astype(F32)
    return (result * cut[5]).astype(BF16)


def ring(
    target_rows, target_pos, decoder_rows, source_pos, out_proj, value_proj, attention, tile_pattern
):
    blocks = lax.axis_size("tgt")
    column = lax.axis_index("tgt")
    src_lane = lax.axis_index("src")
    full_targets, full_sources = (
        lax.all_gather(target_rows, "src", axis=0, tiled=True),
        lax.all_gather(decoder_rows, "src", axis=0, tiled=True),
    )
    tgt_dev = full_targets.shape[0]
    src_dev = full_sources.shape[0]
    sub_rows = decoder_rows.shape[0]
    heads_here = out_proj.shape[0]
    head_dim = out_proj.shape[2]
    groups_here = value_proj.shape[0]
    repeat = heads_here // groups_here
    read_sum = jnp.einsum(
        "td,hde->the",
        full_targets,
        lax.all_gather(out_proj, "tgt", axis=1, tiled=True),
        preferred_element_type=jnp.float32,
    )
    head_reads = read_sum.astype(jnp.bfloat16).reshape(tgt_dev, groups_here, repeat, head_dim)
    values = jnp.einsum("sd,gde->sge", full_sources, value_proj, preferred_element_type=jnp.float32)
    values = values.astype(jnp.bfloat16).reshape(src_dev, groups_here * head_dim)
    attn_table = lax.all_gather(attention, "tgt", axis=1, tiled=True)
    target_attn = jnp.take(attn_table, target_pos, axis=1)
    keyed_attn = jnp.transpose(target_attn, (0, 2, 1))

    def edge_tile(payload, block_index):
        decoder_part, value_part = payload
        key_positions = lax.dynamic_slice_in_dim(source_pos, block_index * src_dev, src_dev)
        weights = jnp.take(keyed_attn, key_positions, axis=1).astype(jnp.float32)
        scores = jnp.einsum(
            "sgd,tgrd->grst",
            value_part.reshape(src_dev, groups_here, head_dim),
            head_reads,
            preferred_element_type=jnp.float32,
        )
        scores = scores.reshape(heads_here, src_dev, tgt_dev)
        mixed_term = jnp.sum(weights * scores, axis=0)
        own_positions = lax.dynamic_slice_in_dim(key_positions, src_lane * sub_rows, sub_rows)
        same_place = (own_positions[:, None] == target_pos[None, :]).astype(jnp.float32)
        direct = (
            jnp.einsum("sd,td->st", decoder_part, full_targets, preferred_element_type=jnp.float32)
            * same_place
        )
        own_rows = lax.dynamic_slice_in_dim(mixed_term, src_lane * sub_rows, sub_rows, 0)
        return lax.dynamic_update_slice_in_dim(
            mixed_term, own_rows + direct, src_lane * sub_rows, 0
        )

    def place_tile(partial_value, payload, block_index):
        kept_flag = tile_pattern[block_index, column]
        piece_tile = edge_tile(payload, block_index) * kept_flag.astype(jnp.float32)
        return lax.dynamic_update_slice_in_dim(partial_value, piece_tile, block_index * src_dev, 0)

    own_block = (decoder_rows, values)
    partial_value = jnp.zeros((blocks * src_dev, tgt_dev), jnp.float32)
    partial_value = place_tile(partial_value, own_block, column)

    def cycle_turn(turn_index, state_carry):
        forward_block, backward_block, running = state_carry
        forward_block = passed_along((forward_block[0], forward_block[1]), "tgt", 1)
        backward_block = passed_along((backward_block[0], backward_block[1]), "tgt", -1)
        running = place_tile(running, forward_block, (column - turn_index) % blocks)
        running = place_tile(running, backward_block, (column + turn_index) % blocks)
        return (forward_block, backward_block, running)

    forward_block, _, partial_value = lax.fori_loop(
        1, blocks // 2, cycle_turn, (own_block, own_block, partial_value)
    )
    forward_block = passed_along((forward_block[0], forward_block[1]), "tgt", 1)
    partial_value = place_tile(partial_value, forward_block, (column - blocks // 2) % blocks)
    summed = lax.psum_scatter(partial_value, "src", scatter_dimension=0, tiled=True)
    return summed.astype(jnp.bfloat16)


def shards(*args):
    target_rows, target_pos, decoder_rows, source_pos, out_proj, value_proj, attention, _ = args
    blocks, lanes = lax.axis_size("tgt"), lax.axis_size("src")
    heads, groups = out_proj.shape[0], value_proj.shape[0]
    fits = (
        blocks == 4
        and lanes == 4
        and out_proj.shape[1] % 128 == 0
        and out_proj.shape[2] == 128
        and heads == 2 * groups
        and groups % 2 == 0
        and source_pos.shape[0] == target_pos.shape[0] == attention.shape[2] == 256
        and target_rows.shape[0] % 16 == 0
        and decoder_rows.shape[0] % 16 == 0
        and attention.shape[1] % 16 == 0
    )
    if not fits:
        return ring(*args)
    return resident(*args)


def solution(mesh):
    return jax.shard_map(
        shards,
        mesh=mesh,
        in_specs=(
            P(("grp", "tgt", "src"), None),
            P(("grp", "tgt")),
            P(("grp", "tgt", "src"), None),
            P("grp"),
            P("src", "tgt", None),
            P("src", None, None),
            P(("grp", "src"), "tgt", None),
            P("grp", None),
        ),
        out_specs=P(("grp", "src"), "tgt"),
        check_vma=False,
    )
```

```python
import functools

import jax
import jax.numpy as jnp
from jax import lax
from jax.experimental import pallas as pl
from jax.experimental.pallas import tpu as pltpu
from jax.sharding import PartitionSpec as P


F32 = jnp.float32
BF16 = jnp.bfloat16
VMEM_BYTES = 24 << 20


def passed_along(value, axis, steps):
    count = lax.axis_size(axis)
    pairs = [(source, (source + steps) % count) for source in range(count)]
    return lax.ppermute(value, axis, pairs)


def swapped(value, axis, bit):
    pairs = [(source, source ^ bit) for source in range(lax.axis_size(axis))]
    return lax.ppermute(value, axis, pairs)


def kernel_call(body, outs, args, flops, moved, scratch=(), smem=(), hbm=()):
    return pl.pallas_call(
        body,
        out_shape=outs,
        in_specs=[
            pl.BlockSpec(
                memory_space=pltpu.SMEM if i in smem else pltpu.HBM if i in hbm else pltpu.VMEM
            )
            for i in range(len(args))
        ],
        out_specs=jax.tree.map(lambda _: pl.BlockSpec(memory_space=pltpu.VMEM), outs),
        scratch_shapes=scratch,
        compiler_params=pltpu.CompilerParams(vmem_limit_bytes=VMEM_BYTES),
        cost_estimate=pl.CostEstimate(flops=flops, bytes_accessed=moved, transcendentals=0),
    )(
        *[
            pltpu.with_memory_space_constraint(arg, pltpu.HBM) if i in hbm else arg
            for i, arg in enumerate(args)
        ]
    )


def aligned(start, size):
    return pl.ds(pl.multiple_of(start, size), size)


def pair_of(ref, first, rows=slice(None)):
    return jnp.concatenate([ref[first, rows, :], ref[first + 1, rows, :]], axis=-1)


def source_row(z, k, block):
    b = z ^ k
    return (b % 2) * (2 * block) + (b // 2) * block


def by_core(positions):
    quarter = positions.shape[1] // 4
    return jnp.concatenate(
        [positions[:, b * quarter : (b + 1) * quarter] for b in (0, 2, 1, 3)], axis=1
    )


def front_kernel(
    targets, sources, attn, spos, tpos, pattern, own, first, second, third, table, kept, held, spots, flags, done
):
    z = lax.axis_index("tgt")
    rows, sub = targets.shape[0], sources.shape[0]
    part = own.shape[1]
    heads, queries, keys = attn.shape
    base = heads * queries

    def columns(index):
        return pl.ds(pl.multiple_of(index * part, 128), part)

    moves = [(attn, held), (spos, spots.at[0]), (tpos, spots.at[1]), (pattern, flags)]
    for k, out in enumerate((first, second, third), 1):
        at = columns(z ^ k)
        moves.append((targets.at[:, at], out.at[pl.ds(0, rows)]))
        moves.append((sources.at[:, at], out.at[pl.ds(rows, sub)]))
    moves.append((targets.at[:, columns(z)], own.at[pl.ds(0, rows)]))
    for i in range(4):
        moves.append((sources.at[:, pl.ds(i * part, part)], own.at[pl.ds(rows + i * sub, sub)]))
    copies = [pltpu.make_async_copy(*ends, done.at[i]) for i, ends in enumerate(moves)]
    for copy in copies:
        copy.start()
    for copy in copies[:4]:
        copy.wait()
    picks = lax.broadcasted_iota(jnp.int32, (keys, spos.shape[1]), 0) == by_core(spots[0])
    picks = picks.astype(F32).astype(BF16)
    table[0:base, :] = jnp.dot(
        held[...].reshape(base, keys), picks, preferred_element_type=F32
    ).astype(BF16)
    table[base:, :] = jnp.broadcast_to(
        spots[1].astype(F32), (table.shape[0] - base, tpos.shape[1])
    ).astype(BF16)
    across = lax.broadcasted_iota(jnp.int32, pattern.shape, 0) == lax.axis_index("src")
    down = lax.broadcasted_iota(jnp.int32, pattern.shape, 1) == z
    flag = jnp.where(across & down, flags[...], 0).astype(F32)
    kept[...] = jnp.broadcast_to(jnp.sum(flag, keepdims=True), kept.shape)
    for copy in copies[4:]:
        copy.wait()


def values_kernel(rows, own, core, far, cross, value, out, held, done):
    s = lax.axis_index("src")
    sub = (own.shape[0] - rows) // 4
    part = own.shape[1]
    pairs = value.shape[0] // 2
    copies = [
        pltpu.make_async_copy(
            value.at[:, pl.ds(i * part, part), :], held.at[:, pl.ds(i * part, part), :], done.at[i]
        )
        for i in range(4)
    ]
    for copy in copies:
        copy.start()
    totals = [None] * pairs
    for i in range(4):
        copies[i].wait()
        at = slice(rows + i * sub, rows + (i + 1) * sub)
        left = jnp.concatenate([ref[at, :] for ref in (own, core, far, cross)], axis=0)
        for pair in range(pairs):
            got = jnp.dot(
                left,
                pair_of(held, 2 * pair, slice(i * part, (i + 1) * part)),
                preferred_element_type=F32,
            )
            totals[pair] = got if i == 0 else totals[pair] + got
    for pair, total in enumerate(totals):
        width = total.shape[1]
        for j in range(4):
            out[aligned((s ^ j) * sub, sub), pair * width : (pair + 1) * width] = total[
                j * sub : (j + 1) * sub, :
            ].astype(BF16)


def reads_kernel(rows, *refs):
    pieces, weight, reads, direct, dec = refs[:16], refs[16], refs[17], refs[18], refs[19]
    z, s = lax.axis_index("tgt"), lax.axis_index("src")
    sub = pieces[4].shape[0] - rows
    block = 4 * sub
    dec[...] = jnp.zeros_like(dec)
    for k in range(4):
        if k:
            piece = pieces[4 * k][rows:, :]
        else:
            piece = pieces[0][aligned(rows + sub * z, sub), :]
        dec[aligned(source_row(z, k, block) + sub * s, sub), :] = piece
    width = 2 * weight.shape[2]
    group = 4 * rows

    def put(k, target, cols, value):
        for j in range(4):
            target[aligned(k * group + (s ^ j) * rows, rows), cols] = value[
                j * rows : (j + 1) * rows
            ].astype(target.dtype)

    lefts = [
        jnp.concatenate([ref[0:rows, :] for ref in pieces[4 * k : 4 * k + 4]], axis=0)
        for k in range(4)
    ]
    for pair in range(weight.shape[0] // 2):
        right = pair_of(weight, 2 * pair)
        for k in range(4):
            got = jnp.dot(lefts[k], right, preferred_element_type=F32)
            put(k, reads, slice(pair * width, (pair + 1) * width), got)
    for k in range(4):
        got = lax.dot_general(
            lefts[k], dec[...], (((1,), (1,)), ((), ())), preferred_element_type=F32
        )
        put(k, direct, slice(0, direct.shape[1]), got)


def scores_kernel(home, first, second, third, reads, out, values):
    z = lax.axis_index("tgt")
    block, width = home.shape
    heads = out.shape[0]
    dim = reads.shape[1] // heads
    for k, ref in enumerate((home, first, second, third)):
        values[aligned(source_row(z, k, block), block), :] = ref[...]
    for group in range(width // dim):
        turned = values[:, group * dim : (group + 1) * dim].astype(F32).T.astype(BF16)
        for head in (2 * group, 2 * group + 1):
            out[head] = jnp.dot(
                reads[:, head * dim : (head + 1) * dim], turned, preferred_element_type=F32
            )


def edges_kernel(heads, queries, shown, home, first, second, third, scores, direct, spos, away, kept):
    tables = (home, first, second, third)
    z, s = lax.axis_index("tgt"), lax.axis_index("src")
    sources = spos.shape[1]
    half = sources // 2
    base = heads * queries
    block = sources // 4
    core = s % 2
    sides = (aligned((1 - core) * half, half), aligned(core * half, half))
    ordered = by_core(spos[...])
    grid_q = jnp.concatenate(
        [
            lax.broadcasted_iota(jnp.int32, (queries, sources), 0) + (z ^ k) * queries
            for k in range(4)
        ],
        axis=0,
    )
    turned = jnp.concatenate([ordered[:, half:], ordered[:, :half]], axis=1)
    picks = (grid_q == jnp.where(core == 0, turned, ordered)).astype(F32).astype(BF16)
    for i, k in enumerate(shown):
        tpos = tables[k][base : base + 16, :].astype(F32)[0:1].astype(jnp.int32)
        hot = (grid_q == tpos).astype(F32).T.astype(BF16)
        here = slice(k * sources, (k + 1) * sources)
        same = jnp.dot(hot, picks, preferred_element_type=F32)
        mixed = [
            same[:, j * half : (j + 1) * half] * direct[here, lanes] for j, lanes in enumerate(sides)
        ]
        for h in range(heads):
            table = jnp.concatenate(
                [
                    jnp.concatenate([t[h * queries : (h + 1) * queries, lanes] for t in tables], axis=0)
                    for lanes in sides
                ],
                axis=1,
            )
            weights = jnp.dot(hot, table, preferred_element_type=F32)
            for j, lanes in enumerate(sides):
                mixed[j] = mixed[j] + weights[:, j * half : (j + 1) * half] * scores[h, here, lanes]
        for out, value in zip((away, kept), mixed):
            value = value.T
            for x in range(2):
                row = jnp.where(s // 2 == x, block, 0)
                out[aligned(row, block), i * sources : (i + 1) * sources] = value[
                    x * block : (x + 1) * block, :
                ]


def resident(
    target_rows, target_pos, decoder_rows, source_pos, out_proj, value_proj, attention, tile_pattern
):
    blocks = lax.axis_size("tgt")
    rows, depth = target_rows.shape
    sub = decoder_rows.shape[0]
    part = depth // blocks
    heads, _, head_dim = out_proj.shape
    groups = value_proj.shape[0]
    queries = attention.shape[1]
    sources = source_pos.shape[0]
    targets = target_pos.shape[0]
    block = sources // blocks

    def shape(*dims, dtype=BF16):
        return jax.ShapeDtypeStruct(dims, dtype)

    spots = source_pos[None, :]
    cut = kernel_call(
        front_kernel,
        (shape(rows + 4 * sub, part),)
        + (shape(rows + sub, part),) * 3
        + (shape(heads * queries + 16, sources), shape(1, targets, dtype=F32)),
        [target_rows, decoder_rows, attention, spots, target_pos[None, :], tile_pattern],
        2 * attention.size * sources,
        target_rows.size * 4,
        [
            pltpu.VMEM(attention.shape, BF16),
            pltpu.VMEM((2, 1, sources), jnp.int32),
            pltpu.VMEM(tile_pattern.shape, jnp.int32),
            pltpu.SemaphoreType.DMA((15,)),
        ],
        hbm=(0, 1, 2, 3, 4, 5),
    )

    def doubled(value):
        second = swapped(value, "tgt", 2)
        return [value, swapped(value, "tgt", 1), second, swapped(second, "tgt", 1)]

    own = [cut[0]] + [swapped(cut[k], "tgt", k) for k in range(1, blocks)]
    far = [swapped(own[k], "src", 2) for k in range(blocks)]
    core = [swapped(own[k], "src", 1) for k in range(blocks)]
    cross = [swapped(far[k], "src", 1) for k in range(blocks)]
    tables = doubled(cut[4])
    values = kernel_call(
        functools.partial(values_kernel, rows),
        shape(block, groups * head_dim),
        [own[0], core[0], far[0], cross[0], value_proj],
        2 * block * depth * groups * head_dim,
        value_proj.size * 2,
        [pltpu.VMEM(value_proj.shape, BF16), pltpu.SemaphoreType.DMA((4,))],
        hbm=(4,),
    )
    values = doubled(values)

    reads, direct = kernel_call(
        functools.partial(reads_kernel, rows),
        (shape(blocks * targets, heads * head_dim), shape(blocks * targets, sources, dtype=F32)),
        [a[k] for k in range(blocks) for a in (own, core, far, cross)] + [out_proj],
        2 * blocks * targets * part * (heads * head_dim + sources),
        out_proj.size * 2,
        [pltpu.VMEM((sources, part), BF16)],
    )
    scores = kernel_call(
        scores_kernel,
        shape(heads, blocks * targets, sources, dtype=F32),
        [*values, reads],
        2 * blocks * targets * sources * heads * head_dim,
        1 << 22,
        [pltpu.VMEM((sources, groups * head_dim), BF16)],
    )

    def edges(shown):
        away, kept = kernel_call(
            functools.partial(edges_kernel, heads, queries, shown),
            (shape(2 * block, len(shown) * targets, dtype=F32),) * 2,
            [*tables, scores, direct, spots],
            len(shown) * targets * sources * sources * heads * 2,
            1 << 22,
        )
        away = swapped(away, "src", 1)
        back = swapped((kept[:block] + away[:block]).astype(BF16), "src", 2)
        return kept[block:] + away[block:] + back.astype(F32)

    distant = edges((2, 3))
    closer = edges((0, 1))
    second = swapped(distant[:, :targets].astype(BF16), "tgt", 2)
    third = swapped(distant[:, targets:].astype(BF16), "tgt", 3)
    first = swapped(closer[:, targets:].astype(BF16), "tgt", 1)
    total = closer[:, :targets]
    for value in (first, second, third):
        total = total + value.astype(F32)
    return (total * cut[5]).astype(BF16)


def ring(
    target_rows, target_pos, decoder_rows, source_pos, out_proj, value_proj, attention, tile_pattern
):
    blocks = lax.axis_size("tgt")
    column = lax.axis_index("tgt")
    src_lane = lax.axis_index("src")
    full_targets, full_sources = (
        lax.all_gather(target_rows, "src", axis=0, tiled=True),
        lax.all_gather(decoder_rows, "src", axis=0, tiled=True),
    )
    tgt_dev = full_targets.shape[0]
    src_dev = full_sources.shape[0]
    sub_rows = decoder_rows.shape[0]
    heads_here = out_proj.shape[0]
    head_dim = out_proj.shape[2]
    groups_here = value_proj.shape[0]
    repeat = heads_here // groups_here
    read_sum = jnp.einsum(
        "td,hde->the",
        full_targets,
        lax.all_gather(out_proj, "tgt", axis=1, tiled=True),
        preferred_element_type=jnp.float32,
    )
    head_reads = read_sum.astype(jnp.bfloat16).reshape(tgt_dev, groups_here, repeat, head_dim)
    values = jnp.einsum("sd,gde->sge", full_sources, value_proj, preferred_element_type=jnp.float32)
    values = values.astype(jnp.bfloat16).reshape(src_dev, groups_here * head_dim)
    attn_table = lax.all_gather(attention, "tgt", axis=1, tiled=True)
    target_attn = jnp.take(attn_table, target_pos, axis=1)
    keyed_attn = jnp.transpose(target_attn, (0, 2, 1))

    def edge_tile(payload, block_index):
        decoder_part, value_part = payload
        key_positions = lax.dynamic_slice_in_dim(source_pos, block_index * src_dev, src_dev)
        weights = jnp.take(keyed_attn, key_positions, axis=1).astype(jnp.float32)
        scores = jnp.einsum(
            "sgd,tgrd->grst",
            value_part.reshape(src_dev, groups_here, head_dim),
            head_reads,
            preferred_element_type=jnp.float32,
        )
        scores = scores.reshape(heads_here, src_dev, tgt_dev)
        mixed_term = jnp.sum(weights * scores, axis=0)
        own_positions = lax.dynamic_slice_in_dim(key_positions, src_lane * sub_rows, sub_rows)
        same_place = (own_positions[:, None] == target_pos[None, :]).astype(jnp.float32)
        direct = (
            jnp.einsum("sd,td->st", decoder_part, full_targets, preferred_element_type=jnp.float32)
            * same_place
        )
        own_rows = lax.dynamic_slice_in_dim(mixed_term, src_lane * sub_rows, sub_rows, 0)
        return lax.dynamic_update_slice_in_dim(
            mixed_term, own_rows + direct, src_lane * sub_rows, 0
        )

    def place_tile(partial_value, payload, block_index):
        kept_flag = tile_pattern[block_index, column]
        piece_tile = edge_tile(payload, block_index) * kept_flag.astype(jnp.float32)
        return lax.dynamic_update_slice_in_dim(partial_value, piece_tile, block_index * src_dev, 0)

    own_block = (decoder_rows, values)
    partial_value = jnp.zeros((blocks * src_dev, tgt_dev), jnp.float32)
    partial_value = place_tile(partial_value, own_block, column)

    def cycle_turn(turn_index, state_carry):
        forward_block, backward_block, running = state_carry
        forward_block = passed_along((forward_block[0], forward_block[1]), "tgt", 1)
        backward_block = passed_along((backward_block[0], backward_block[1]), "tgt", -1)
        running = place_tile(running, forward_block, (column - turn_index) % blocks)
        running = place_tile(running, backward_block, (column + turn_index) % blocks)
        return (forward_block, backward_block, running)

    forward_block, _, partial_value = lax.fori_loop(
        1, blocks // 2, cycle_turn, (own_block, own_block, partial_value)
    )
    forward_block = passed_along((forward_block[0], forward_block[1]), "tgt", 1)
    partial_value = place_tile(partial_value, forward_block, (column - blocks // 2) % blocks)
    summed = lax.psum_scatter(partial_value, "src", scatter_dimension=0, tiled=True)
    return summed.astype(jnp.bfloat16)


def shards(*args):
    target_rows, target_pos, decoder_rows, source_pos, out_proj, value_proj, attention, _ = args
    blocks, lanes = lax.axis_size("tgt"), lax.axis_size("src")
    heads, groups = out_proj.shape[0], value_proj.shape[0]
    fits = (
        blocks == 4
        and lanes == 4
        and out_proj.shape[1] % 128 == 0
        and out_proj.shape[2] == 128
        and heads == 2 * groups
        and groups % 2 == 0
        and source_pos.shape[0] == target_pos.shape[0] == attention.shape[2] == 256
        and target_rows.shape[0] % 16 == 0
        and decoder_rows.shape[0] % 16 == 0
        and attention.shape[1] % 16 == 0
    )
    if not fits:
        return ring(*args)
    return resident(*args)


def solution(mesh):
    return jax.shard_map(
        shards,
        mesh=mesh,
        in_specs=(
            P(("grp", "tgt", "src"), None),
            P(("grp", "tgt")),
            P(("grp", "tgt", "src"), None),
            P("grp"),
            P("src", "tgt", None),
            P("src", None, None),
            P(("grp", "src"), "tgt", None),
            P("grp", None),
        ),
        out_specs=P(("grp", "src"), "tgt"),
        check_vma=False,
    )
```

```python
import functools

import jax
import jax.numpy as jnp
from jax import lax
from jax.experimental import pallas as pl
from jax.experimental.pallas import tpu as pltpu
from jax.sharding import PartitionSpec as P


F32 = jnp.float32
BF16 = jnp.bfloat16
VMEM_BYTES = 24 << 20


def passed_along(value, axis, steps):
    count = lax.axis_size(axis)
    pairs = [(source, (source + steps) % count) for source in range(count)]
    return lax.ppermute(value, axis, pairs)


def swapped(value, axis, bit):
    pairs = [(source, source ^ bit) for source in range(lax.axis_size(axis))]
    return lax.ppermute(value, axis, pairs)


def kernel_call(body, outs, args, flops, moved, scratch=(), smem=(), hbm=()):
    return pl.pallas_call(
        body,
        out_shape=outs,
        in_specs=[
            pl.BlockSpec(
                memory_space=pltpu.SMEM if i in smem else pltpu.HBM if i in hbm else pltpu.VMEM
            )
            for i in range(len(args))
        ],
        out_specs=jax.tree.map(lambda _: pl.BlockSpec(memory_space=pltpu.VMEM), outs),
        scratch_shapes=scratch,
        compiler_params=pltpu.CompilerParams(vmem_limit_bytes=VMEM_BYTES),
        cost_estimate=pl.CostEstimate(flops=flops, bytes_accessed=moved, transcendentals=0),
    )(
        *[
            pltpu.with_memory_space_constraint(arg, pltpu.HBM) if i in hbm else arg
            for i, arg in enumerate(args)
        ]
    )


def aligned(start, size):
    return pl.ds(pl.multiple_of(start, size), size)


def pair_of(ref, first, rows=slice(None)):
    return jnp.concatenate([ref[first, rows, :], ref[first + 1, rows, :]], axis=-1)


def source_row(z, k, block):
    b = z ^ k
    return (b % 2) * (2 * block) + (b // 2) * block


def by_core(positions):
    quarter = positions.shape[1] // 4
    return jnp.concatenate(
        [positions[:, b * quarter : (b + 1) * quarter] for b in (0, 2, 1, 3)], axis=1
    )


def front_kernel(
    targets, sources, attn, spos, tpos, pattern, own, first, second, third, upper, lower, kept, held, spots, flags, done
):
    z = lax.axis_index("tgt")
    rows, sub = targets.shape[0], sources.shape[0]
    part = own.shape[1]
    heads, queries, keys = attn.shape
    base = heads * queries

    def columns(index):
        return pl.ds(pl.multiple_of(index * part, 128), part)

    moves = [(attn, held), (spos, spots.at[0]), (tpos, spots.at[1]), (pattern, flags)]
    for k, out in enumerate((first, second, third), 1):
        at = columns(z ^ k)
        moves.append((targets.at[:, at], out.at[pl.ds(0, rows)]))
        moves.append((sources.at[:, at], out.at[pl.ds(rows, sub)]))
    moves.append((targets.at[:, columns(z)], own.at[pl.ds(0, rows)]))
    for i in range(4):
        moves.append((sources.at[:, pl.ds(i * part, part)], own.at[pl.ds(rows + i * sub, sub)]))
    copies = [pltpu.make_async_copy(*ends, done.at[i]) for i, ends in enumerate(moves)]
    for copy in copies:
        copy.start()
    for copy in copies[:4]:
        copy.wait()
    picks = lax.broadcasted_iota(jnp.int32, (keys, spos.shape[1]), 0) == by_core(spots[0])
    picks = picks.astype(F32).astype(BF16)
    table = jnp.dot(held[...].reshape(base, keys), picks, preferred_element_type=F32).astype(BF16)
    cut = lower.shape[0]
    lower[...] = table[base - cut :]
    upper[0 : base - cut, :] = table[: base - cut]
    upper[base - cut :, :] = jnp.broadcast_to(
        spots[1].astype(F32), (upper.shape[0] + cut - base, tpos.shape[1])
    ).astype(BF16)
    across = lax.broadcasted_iota(jnp.int32, pattern.shape, 0) == lax.axis_index("src")
    down = lax.broadcasted_iota(jnp.int32, pattern.shape, 1) == z
    flag = jnp.where(across & down, flags[...], 0).astype(F32)
    kept[...] = jnp.broadcast_to(jnp.sum(flag, keepdims=True), kept.shape)
    for copy in copies[4:]:
        copy.wait()


def values_kernel(rows, own, core, far, cross, value, out, held, done):
    s = lax.axis_index("src")
    sub = (own.shape[0] - rows) // 4
    part = own.shape[1]
    pairs = value.shape[0] // 2
    copies = [
        pltpu.make_async_copy(
            value.at[:, pl.ds(i * part, part), :], held.at[:, pl.ds(i * part, part), :], done.at[i]
        )
        for i in range(4)
    ]
    for copy in copies:
        copy.start()
    totals = [None] * pairs
    for i in range(4):
        copies[i].wait()
        at = slice(rows + i * sub, rows + (i + 1) * sub)
        left = jnp.concatenate([ref[at, :] for ref in (own, core, far, cross)], axis=0)
        for pair in range(pairs):
            got = jnp.dot(
                left,
                pair_of(held, 2 * pair, slice(i * part, (i + 1) * part)),
                preferred_element_type=F32,
            )
            totals[pair] = got if i == 0 else totals[pair] + got
    for pair, total in enumerate(totals):
        width = total.shape[1]
        for j in range(4):
            out[aligned((s ^ j) * sub, sub), pair * width : (pair + 1) * width] = total[
                j * sub : (j + 1) * sub, :
            ].astype(BF16)


def stacked(rows, pieces):
    return jnp.concatenate([ref[0:rows, :] for ref in pieces], axis=0)


def put(rows, target, start, cols, value):
    s = lax.axis_index("src")
    for j in range(4):
        target[aligned(start + (s ^ j) * rows, rows), cols] = value[
            j * rows : (j + 1) * rows
        ].astype(target.dtype)


def put_reads(rows, lefts, weight, reads):
    width = 2 * weight.shape[2]
    for pair in range(weight.shape[0] // 2):
        right = pair_of(weight, 2 * pair)
        for i, left in enumerate(lefts):
            got = jnp.dot(left, right, preferred_element_type=F32)
            put(rows, reads, 4 * i * rows, slice(pair * width, (pair + 1) * width), got)


def near_kernel(rows, *refs):
    pieces, weight, reads = refs[:8], refs[8], refs[9]
    put_reads(rows, [stacked(rows, pieces[4 * i : 4 * i + 4]) for i in range(2)], weight, reads)


def far_kernel(rows, *refs):
    pieces, weight, reads, direct, dec = refs[:16], refs[16], refs[17], refs[18], refs[19]
    z, s = lax.axis_index("tgt"), lax.axis_index("src")
    sub = pieces[4].shape[0] - rows
    block = 4 * sub
    dec[...] = jnp.zeros_like(dec)
    for k in range(4):
        if k:
            piece = pieces[4 * k][rows:, :]
        else:
            piece = pieces[0][aligned(rows + sub * z, sub), :]
        dec[aligned(source_row(z, k, block) + sub * s, sub), :] = piece
    lefts = [stacked(rows, pieces[4 * k : 4 * k + 4]) for k in range(4)]
    put_reads(rows, lefts[2:], weight, reads)
    for k in range(4):
        got = lax.dot_general(
            lefts[k], dec[...], (((1,), (1,)), ((), ())), preferred_element_type=F32
        )
        put(rows, direct, 4 * k * rows, slice(0, direct.shape[1]), got)


def scores_kernel(home, first, second, third, reads, out, values):
    z = lax.axis_index("tgt")
    block, width = home.shape
    heads = out.shape[0]
    dim = reads.shape[1] // heads
    for k, ref in enumerate((home, first, second, third)):
        values[aligned(source_row(z, k, block), block), :] = ref[...]
    for group in range(width // dim):
        turned = values[:, group * dim : (group + 1) * dim].astype(F32).T.astype(BF16)
        for head in (2 * group, 2 * group + 1):
            out[head] = jnp.dot(
                reads[:, head * dim : (head + 1) * dim], turned, preferred_element_type=F32
            )


def edges_kernel(heads, queries, shown, *refs):
    uppers, lowers = refs[0:4], refs[4:8]
    scores, direct, spos, away, kept = refs[8:]
    z, s = lax.axis_index("tgt"), lax.axis_index("src")
    sources = spos.shape[1]
    half = sources // 2
    base = heads // 2 * queries
    block = sources // 4
    core = s % 2
    sides = (aligned((1 - core) * half, half), aligned(core * half, half))
    ordered = by_core(spos[...])
    grid_q = jnp.concatenate(
        [
            lax.broadcasted_iota(jnp.int32, (queries, sources), 0) + (z ^ k) * queries
            for k in range(4)
        ],
        axis=0,
    )
    turned = jnp.concatenate([ordered[:, half:], ordered[:, :half]], axis=1)
    picks = (grid_q == jnp.where(core == 0, turned, ordered)).astype(F32).astype(BF16)
    for i, k in enumerate(shown):
        tpos = uppers[k][base : base + 16, :].astype(F32)[0:1].astype(jnp.int32)
        hot = (grid_q == tpos).astype(F32).T.astype(BF16)
        here = slice(k * sources, (k + 1) * sources)
        there = slice(i * sources, (i + 1) * sources)
        same = jnp.dot(hot, picks, preferred_element_type=F32)
        mixed = [
            same[:, j * half : (j + 1) * half] * direct[here, lanes] for j, lanes in enumerate(sides)
        ]
        for h in range(heads):
            tables = uppers if h < heads // 2 else lowers
            at = h % (heads // 2) * queries
            table = jnp.concatenate(
                [
                    jnp.concatenate([t[at : at + queries, lanes] for t in tables], axis=0)
                    for lanes in sides
                ],
                axis=1,
            )
            weights = jnp.dot(hot, table, preferred_element_type=F32)
            for j, lanes in enumerate(sides):
                mixed[j] = mixed[j] + weights[:, j * half : (j + 1) * half] * scores[h, there, lanes]
        for out, value in zip((away, kept), mixed):
            value = value.T
            for x in range(2):
                row = jnp.where(s // 2 == x, block, 0)
                out[aligned(row, block), i * sources : (i + 1) * sources] = value[
                    x * block : (x + 1) * block, :
                ]


def resident(
    target_rows, target_pos, decoder_rows, source_pos, out_proj, value_proj, attention, tile_pattern
):
    blocks = lax.axis_size("tgt")
    rows, depth = target_rows.shape
    sub = decoder_rows.shape[0]
    part = depth // blocks
    heads, _, head_dim = out_proj.shape
    groups = value_proj.shape[0]
    queries = attention.shape[1]
    sources = source_pos.shape[0]
    targets = target_pos.shape[0]
    block = sources // blocks

    def shape(*dims, dtype=BF16):
        return jax.ShapeDtypeStruct(dims, dtype)

    spots = source_pos[None, :]
    cut = kernel_call(
        front_kernel,
        (shape(rows + 4 * sub, part),)
        + (shape(rows + sub, part),) * 3
        + (
            shape(heads // 2 * queries + 16, sources),
            shape(heads // 2 * queries, sources),
            shape(1, targets, dtype=F32),
        ),
        [target_rows, decoder_rows, attention, spots, target_pos[None, :], tile_pattern],
        2 * attention.size * sources,
        target_rows.size * 4,
        [
            pltpu.VMEM(attention.shape, BF16),
            pltpu.VMEM((2, 1, sources), jnp.int32),
            pltpu.VMEM(tile_pattern.shape, jnp.int32),
            pltpu.SemaphoreType.DMA((15,)),
        ],
        hbm=(0, 1, 2, 3, 4, 5),
    )

    def doubled(value):
        second = swapped(value, "tgt", 2)
        return [value, swapped(value, "tgt", 1), second, swapped(second, "tgt", 1)]

    own = [cut[0]] + [swapped(cut[k], "tgt", k) for k in range(1, blocks)]
    far = [swapped(own[k], "src", 2) for k in range(blocks)]
    core = [swapped(own[k], "src", 1) for k in range(blocks)]
    cross = [swapped(far[k], "src", 1) for k in range(blocks)]
    tables = doubled(cut[4]) + doubled(cut[5])
    values = kernel_call(
        functools.partial(values_kernel, rows),
        shape(block, groups * head_dim),
        [own[0], core[0], far[0], cross[0], value_proj],
        2 * block * depth * groups * head_dim,
        value_proj.size * 2,
        [pltpu.VMEM(value_proj.shape, BF16), pltpu.SemaphoreType.DMA((4,))],
        hbm=(4,),
    )
    values = doubled(values)

    groups_of = [a[k] for k in range(blocks) for a in (own, core, far, cross)]
    wide = heads * head_dim
    near = kernel_call(
        functools.partial(near_kernel, rows),
        shape(2 * targets, wide),
        [*groups_of[:8], out_proj],
        4 * targets * part * wide,
        out_proj.size * 2,
    )
    distant, direct = kernel_call(
        functools.partial(far_kernel, rows),
        (shape(2 * targets, wide), shape(blocks * targets, sources, dtype=F32)),
        [*groups_of, out_proj],
        4 * targets * part * (wide + 2 * sources),
        out_proj.size * 2,
        [pltpu.VMEM((sources, part), BF16)],
    )

    def scored(reads):
        return kernel_call(
            scores_kernel,
            shape(heads, 2 * targets, sources, dtype=F32),
            [*values, reads],
            4 * targets * sources * heads * head_dim,
            1 << 21,
            [pltpu.VMEM((sources, groups * head_dim), BF16)],
        )

    scores = {"a": scored(distant), "b": scored(near)}

    def edges(name, shown):
        away, kept = kernel_call(
            functools.partial(edges_kernel, heads, queries, shown),
            (shape(2 * block, len(shown) * targets, dtype=F32),) * 2,
            [*tables, scores[name], direct, spots],
            len(shown) * targets * sources * sources * heads * 2,
            1 << 22,
        )
        away = swapped(away, "src", 1)
        back = swapped((kept[:block] + away[:block]).astype(BF16), "src", 2)
        return kept[block:] + away[block:] + back.astype(F32)

    outer = edges("a", (2, 3))
    closer = edges("b", (0, 1))
    second = swapped(outer[:, :targets].astype(BF16), "tgt", 2)
    third = swapped(outer[:, targets:].astype(BF16), "tgt", 3)
    first = swapped(closer[:, targets:].astype(BF16), "tgt", 1)
    total = closer[:, :targets]
    for value in (first, second, third):
        total = total + value.astype(F32)
    return (total * cut[6]).astype(BF16)


def ring(
    target_rows, target_pos, decoder_rows, source_pos, out_proj, value_proj, attention, tile_pattern
):
    blocks = lax.axis_size("tgt")
    column = lax.axis_index("tgt")
    src_lane = lax.axis_index("src")
    full_targets, full_sources = (
        lax.all_gather(target_rows, "src", axis=0, tiled=True),
        lax.all_gather(decoder_rows, "src", axis=0, tiled=True),
    )
    tgt_dev = full_targets.shape[0]
    src_dev = full_sources.shape[0]
    sub_rows = decoder_rows.shape[0]
    heads_here = out_proj.shape[0]
    head_dim = out_proj.shape[2]
    groups_here = value_proj.shape[0]
    repeat = heads_here // groups_here
    read_sum = jnp.einsum(
        "td,hde->the",
        full_targets,
        lax.all_gather(out_proj, "tgt", axis=1, tiled=True),
        preferred_element_type=jnp.float32,
    )
    head_reads = read_sum.astype(jnp.bfloat16).reshape(tgt_dev, groups_here, repeat, head_dim)
    values = jnp.einsum("sd,gde->sge", full_sources, value_proj, preferred_element_type=jnp.float32)
    values = values.astype(jnp.bfloat16).reshape(src_dev, groups_here * head_dim)
    attn_table = lax.all_gather(attention, "tgt", axis=1, tiled=True)
    target_attn = jnp.take(attn_table, target_pos, axis=1)
    keyed_attn = jnp.transpose(target_attn, (0, 2, 1))

    def edge_tile(payload, block_index):
        decoder_part, value_part = payload
        key_positions = lax.dynamic_slice_in_dim(source_pos, block_index * src_dev, src_dev)
        weights = jnp.take(keyed_attn, key_positions, axis=1).astype(jnp.float32)
        scores = jnp.einsum(
            "sgd,tgrd->grst",
            value_part.reshape(src_dev, groups_here, head_dim),
            head_reads,
            preferred_element_type=jnp.float32,
        )
        scores = scores.reshape(heads_here, src_dev, tgt_dev)
        mixed_term = jnp.sum(weights * scores, axis=0)
        own_positions = lax.dynamic_slice_in_dim(key_positions, src_lane * sub_rows, sub_rows)
        same_place = (own_positions[:, None] == target_pos[None, :]).astype(jnp.float32)
        direct = (
            jnp.einsum("sd,td->st", decoder_part, full_targets, preferred_element_type=jnp.float32)
            * same_place
        )
        own_rows = lax.dynamic_slice_in_dim(mixed_term, src_lane * sub_rows, sub_rows, 0)
        return lax.dynamic_update_slice_in_dim(
            mixed_term, own_rows + direct, src_lane * sub_rows, 0
        )

    def place_tile(partial_value, payload, block_index):
        kept_flag = tile_pattern[block_index, column]
        piece_tile = edge_tile(payload, block_index) * kept_flag.astype(jnp.float32)
        return lax.dynamic_update_slice_in_dim(partial_value, piece_tile, block_index * src_dev, 0)

    own_block = (decoder_rows, values)
    partial_value = jnp.zeros((blocks * src_dev, tgt_dev), jnp.float32)
    partial_value = place_tile(partial_value, own_block, column)

    def cycle_turn(turn_index, state_carry):
        forward_block, backward_block, running = state_carry
        forward_block = passed_along((forward_block[0], forward_block[1]), "tgt", 1)
        backward_block = passed_along((backward_block[0], backward_block[1]), "tgt", -1)
        running = place_tile(running, forward_block, (column - turn_index) % blocks)
        running = place_tile(running, backward_block, (column + turn_index) % blocks)
        return (forward_block, backward_block, running)

    forward_block, _, partial_value = lax.fori_loop(
        1, blocks // 2, cycle_turn, (own_block, own_block, partial_value)
    )
    forward_block = passed_along((forward_block[0], forward_block[1]), "tgt", 1)
    partial_value = place_tile(partial_value, forward_block, (column - blocks // 2) % blocks)
    summed = lax.psum_scatter(partial_value, "src", scatter_dimension=0, tiled=True)
    return summed.astype(jnp.bfloat16)


def shards(*args):
    target_rows, target_pos, decoder_rows, source_pos, out_proj, value_proj, attention, _ = args
    blocks, lanes = lax.axis_size("tgt"), lax.axis_size("src")
    heads, groups = out_proj.shape[0], value_proj.shape[0]
    fits = (
        blocks == 4
        and lanes == 4
        and out_proj.shape[1] % 128 == 0
        and out_proj.shape[2] == 128
        and heads == 2 * groups
        and groups % 2 == 0
        and source_pos.shape[0] == target_pos.shape[0] == attention.shape[2] == 256
        and target_rows.shape[0] % 16 == 0
        and decoder_rows.shape[0] % 16 == 0
        and attention.shape[1] % 16 == 0
    )
    if not fits:
        return ring(*args)
    return resident(*args)


def solution(mesh):
    return jax.shard_map(
        shards,
        mesh=mesh,
        in_specs=(
            P(("grp", "tgt", "src"), None),
            P(("grp", "tgt")),
            P(("grp", "tgt", "src"), None),
            P("grp"),
            P("src", "tgt", None),
            P("src", None, None),
            P(("grp", "src"), "tgt", None),
            P("grp", None),
        ),
        out_specs=P(("grp", "src"), "tgt"),
        check_vma=False,
    )
```

```python
import functools

import jax
import jax.numpy as jnp
from jax import lax
from jax.experimental import pallas as pl
from jax.experimental.pallas import tpu as pltpu
from jax.sharding import PartitionSpec as P


F32 = jnp.float32
BF16 = jnp.bfloat16
VMEM_BYTES = 24 << 20


def passed_along(value, axis, steps):
    count = lax.axis_size(axis)
    pairs = [(source, (source + steps) % count) for source in range(count)]
    return lax.ppermute(value, axis, pairs)


def swapped(value, axis, bit):
    pairs = [(source, source ^ bit) for source in range(lax.axis_size(axis))]
    return lax.ppermute(value, axis, pairs)


def kernel_call(body, outs, args, flops, moved, scratch=(), smem=(), hbm=()):
    return pl.pallas_call(
        body,
        out_shape=outs,
        in_specs=[
            pl.BlockSpec(
                memory_space=pltpu.SMEM if i in smem else pltpu.HBM if i in hbm else pltpu.VMEM
            )
            for i in range(len(args))
        ],
        out_specs=jax.tree.map(lambda _: pl.BlockSpec(memory_space=pltpu.VMEM), outs),
        scratch_shapes=scratch,
        compiler_params=pltpu.CompilerParams(vmem_limit_bytes=VMEM_BYTES),
        cost_estimate=pl.CostEstimate(flops=flops, bytes_accessed=moved, transcendentals=0),
    )(
        *[
            pltpu.with_memory_space_constraint(arg, pltpu.HBM) if i in hbm else arg
            for i, arg in enumerate(args)
        ]
    )


def aligned(start, size):
    return pl.ds(pl.multiple_of(start, size), size)


def pair_of(ref, first, rows=slice(None)):
    return jnp.concatenate([ref[first, rows, :], ref[first + 1, rows, :]], axis=-1)


def source_row(z, k, block):
    b = z ^ k
    return (b % 2) * (2 * block) + (b // 2) * block


def by_core(positions):
    quarter = positions.shape[1] // 4
    return jnp.concatenate(
        [positions[:, b * quarter : (b + 1) * quarter] for b in (0, 2, 1, 3)], axis=1
    )


def front_kernel(
    targets, sources, attn, spos, tpos, pattern, own, first, second, third, upper, lower, kept, held, spots, flags, done
):
    z = lax.axis_index("tgt")
    rows, sub = targets.shape[0], sources.shape[0]
    part = own.shape[1]
    heads, queries, keys = attn.shape
    base = heads * queries

    def columns(index):
        return pl.ds(pl.multiple_of(index * part, 128), part)

    moves = [(attn, held), (spos, spots.at[0]), (tpos, spots.at[1]), (pattern, flags)]
    for k, out in enumerate((first, second, third), 1):
        at = columns(z ^ k)
        moves.append((targets.at[:, at], out.at[pl.ds(0, rows)]))
        moves.append((sources.at[:, at], out.at[pl.ds(rows, sub)]))
    moves.append((targets.at[:, columns(z)], own.at[pl.ds(0, rows)]))
    for i in range(4):
        moves.append((sources.at[:, pl.ds(i * part, part)], own.at[pl.ds(rows + i * sub, sub)]))
    copies = [pltpu.make_async_copy(*ends, done.at[i]) for i, ends in enumerate(moves)]
    for copy in copies:
        copy.start()
    for copy in copies[:4]:
        copy.wait()
    picks = lax.broadcasted_iota(jnp.int32, (keys, spos.shape[1]), 0) == by_core(spots[0])
    picks = picks.astype(F32).astype(BF16)
    table = jnp.dot(held[...].reshape(base, keys), picks, preferred_element_type=F32).astype(BF16)
    cut = lower.shape[0]
    lower[...] = table[base - cut :]
    upper[0 : base - cut, :] = table[: base - cut]
    upper[base - cut :, :] = jnp.broadcast_to(
        spots[1].astype(F32), (upper.shape[0] + cut - base, tpos.shape[1])
    ).astype(BF16)
    across = lax.broadcasted_iota(jnp.int32, pattern.shape, 0) == lax.axis_index("src")
    down = lax.broadcasted_iota(jnp.int32, pattern.shape, 1) == z
    flag = jnp.where(across & down, flags[...], 0).astype(F32)
    kept[...] = jnp.broadcast_to(jnp.sum(flag, keepdims=True), kept.shape)
    for copy in copies[4:]:
        copy.wait()


def values_kernel(rows, own, core, far, cross, value, out, held, done):
    s = lax.axis_index("src")
    sub = (own.shape[0] - rows) // 4
    part = own.shape[1]
    pairs = value.shape[0] // 2
    copies = [
        pltpu.make_async_copy(
            value.at[:, pl.ds(i * part, part), :], held.at[:, pl.ds(i * part, part), :], done.at[i]
        )
        for i in range(4)
    ]
    for copy in copies:
        copy.start()
    totals = [None] * pairs
    for i in range(4):
        copies[i].wait()
        at = slice(rows + i * sub, rows + (i + 1) * sub)
        left = jnp.concatenate([ref[at, :] for ref in (own, core, far, cross)], axis=0)
        for pair in range(pairs):
            got = jnp.dot(
                left,
                pair_of(held, 2 * pair, slice(i * part, (i + 1) * part)),
                preferred_element_type=F32,
            )
            totals[pair] = got if i == 0 else totals[pair] + got
    for pair, total in enumerate(totals):
        width = total.shape[1]
        for j in range(4):
            out[aligned((s ^ j) * sub, sub), pair * width : (pair + 1) * width] = total[
                j * sub : (j + 1) * sub, :
            ].astype(BF16)


def stacked(rows, pieces):
    return jnp.concatenate([ref[0:rows, :] for ref in pieces], axis=0)


def put(rows, target, start, cols, value):
    s = lax.axis_index("src")
    for j in range(4):
        target[aligned(start + (s ^ j) * rows, rows), cols] = value[
            j * rows : (j + 1) * rows
        ].astype(target.dtype)


def put_reads(rows, lefts, weight, reads):
    width = 2 * weight.shape[2]
    for pair in range(weight.shape[0] // 2):
        right = pair_of(weight, 2 * pair)
        for i, left in enumerate(lefts):
            got = jnp.dot(left, right, preferred_element_type=F32)
            put(rows, reads, 4 * i * rows, slice(pair * width, (pair + 1) * width), got)


def near_kernel(rows, *refs):
    pieces, weight, reads = refs[:8], refs[8], refs[9]
    put_reads(rows, [stacked(rows, pieces[4 * i : 4 * i + 4]) for i in range(2)], weight, reads)


def far_kernel(rows, *refs):
    pieces, weight, reads, direct, dec = refs[:16], refs[16], refs[17], refs[18], refs[19]
    z, s = lax.axis_index("tgt"), lax.axis_index("src")
    sub = pieces[4].shape[0] - rows
    block = 4 * sub
    dec[...] = jnp.zeros_like(dec)
    for k in range(4):
        if k:
            piece = pieces[4 * k][rows:, :]
        else:
            piece = pieces[0][aligned(rows + sub * z, sub), :]
        dec[aligned(source_row(z, k, block) + sub * s, sub), :] = piece
    lefts = [stacked(rows, pieces[4 * k : 4 * k + 4]) for k in range(4)]
    put_reads(rows, lefts[2:], weight, reads)
    for k in range(4):
        got = lax.dot_general(
            lefts[k], dec[...], (((1,), (1,)), ((), ())), preferred_element_type=F32
        )
        put(rows, direct, 4 * k * rows, slice(0, direct.shape[1]), got)


def scores_kernel(home, first, second, third, reads, out, values):
    z = lax.axis_index("tgt")
    block, width = home.shape
    heads = out.shape[0]
    dim = reads.shape[1] // heads
    for k, ref in enumerate((home, first, second, third)):
        values[aligned(source_row(z, k, block), block), :] = ref[...]
    for group in range(width // dim):
        turned = values[:, group * dim : (group + 1) * dim].astype(F32).T.astype(BF16)
        for head in (2 * group, 2 * group + 1):
            out[head] = jnp.dot(
                reads[:, head * dim : (head + 1) * dim], turned, preferred_element_type=F32
            )


def edges_kernel(heads, queries, shown, *refs):
    uppers, lowers = refs[0:4], refs[4:8]
    scores, direct, spos, away, kept = refs[8:]
    z, s = lax.axis_index("tgt"), lax.axis_index("src")
    sources = spos.shape[1]
    half = sources // 2
    base = heads // 2 * queries
    block = sources // 4
    core = s % 2
    sides = (aligned((1 - core) * half, half), aligned(core * half, half))
    ordered = by_core(spos[...])
    grid_q = jnp.concatenate(
        [
            lax.broadcasted_iota(jnp.int32, (queries, sources), 0) + (z ^ k) * queries
            for k in range(4)
        ],
        axis=0,
    )
    turned = jnp.concatenate([ordered[:, half:], ordered[:, :half]], axis=1)
    picks = (grid_q == jnp.where(core == 0, turned, ordered)).astype(F32).astype(BF16)
    for i, k in enumerate(shown):
        tpos = uppers[k][base : base + 16, :].astype(F32)[0:1].astype(jnp.int32)
        hot = (grid_q == tpos).astype(F32).T.astype(BF16)
        here = slice(k * sources, (k + 1) * sources)
        there = slice(i * sources, (i + 1) * sources)
        same = jnp.dot(hot, picks, preferred_element_type=F32)
        mixed = [
            same[:, j * half : (j + 1) * half] * direct[here, lanes] for j, lanes in enumerate(sides)
        ]
        for h in range(heads):
            tables = uppers if h < heads // 2 else lowers
            at = h % (heads // 2) * queries
            table = jnp.concatenate(
                [
                    jnp.concatenate([t[at : at + queries, lanes] for t in tables], axis=0)
                    for lanes in sides
                ],
                axis=1,
            )
            weights = jnp.dot(hot, table, preferred_element_type=F32)
            for j, lanes in enumerate(sides):
                mixed[j] = mixed[j] + weights[:, j * half : (j + 1) * half] * scores[h, there, lanes]
        for out, value in zip((away, kept), mixed):
            value = value.T
            for x in range(2):
                row = jnp.where(s // 2 == x, block, 0)
                out[aligned(row, block), i * sources : (i + 1) * sources] = value[
                    x * block : (x + 1) * block, :
                ]


def resident(
    target_rows, target_pos, decoder_rows, source_pos, out_proj, value_proj, attention, tile_pattern
):
    blocks = lax.axis_size("tgt")
    rows, depth = target_rows.shape
    sub = decoder_rows.shape[0]
    part = depth // blocks
    heads, _, head_dim = out_proj.shape
    groups = value_proj.shape[0]
    queries = attention.shape[1]
    sources = source_pos.shape[0]
    targets = target_pos.shape[0]
    block = sources // blocks

    def shape(*dims, dtype=BF16):
        return jax.ShapeDtypeStruct(dims, dtype)

    spots = source_pos[None, :]
    cut = kernel_call(
        front_kernel,
        (shape(rows + 4 * sub, part),)
        + (shape(rows + sub, part),) * 3
        + (
            shape(heads // 2 * queries + 16, sources),
            shape(heads // 2 * queries, sources),
            shape(1, targets, dtype=F32),
        ),
        [target_rows, decoder_rows, attention, spots, target_pos[None, :], tile_pattern],
        2 * attention.size * sources,
        target_rows.size * 4,
        [
            pltpu.VMEM(attention.shape, BF16),
            pltpu.VMEM((2, 1, sources), jnp.int32),
            pltpu.VMEM(tile_pattern.shape, jnp.int32),
            pltpu.SemaphoreType.DMA((15,)),
        ],
        hbm=(0, 1, 2, 3, 4, 5),
    )

    def doubled(value):
        second = swapped(value, "tgt", 2)
        return [value, swapped(value, "tgt", 1), second, swapped(second, "tgt", 1)]

    own = [cut[0]] + [swapped(cut[k], "tgt", k) for k in range(1, blocks)]
    far = [swapped(own[k], "src", 2) for k in range(blocks)]
    core = [swapped(own[k], "src", 1) for k in range(blocks)]
    cross = [swapped(far[k], "src", 1) for k in range(blocks)]
    tables = doubled(cut[4]) + doubled(cut[5])
    values = kernel_call(
        functools.partial(values_kernel, rows),
        shape(block, groups * head_dim),
        [own[0], core[0], far[0], cross[0], value_proj],
        2 * block * depth * groups * head_dim,
        value_proj.size * 2,
        [pltpu.VMEM(value_proj.shape, BF16), pltpu.SemaphoreType.DMA((4,))],
        hbm=(4,),
    )
    values = doubled(values)

    groups_of = [a[k] for k in range(blocks) for a in (own, core, far, cross)]
    wide = heads * head_dim
    near = kernel_call(
        functools.partial(near_kernel, rows),
        shape(2 * targets, wide),
        [*groups_of[:8], out_proj],
        4 * targets * part * wide,
        out_proj.size * 2,
    )
    distant, direct = kernel_call(
        functools.partial(far_kernel, rows),
        (shape(2 * targets, wide), shape(blocks * targets, sources, dtype=F32)),
        [*groups_of, out_proj],
        4 * targets * part * (wide + 2 * sources),
        out_proj.size * 2,
        [pltpu.VMEM((sources, part), BF16)],
    )

    def scored(reads):
        return kernel_call(
            scores_kernel,
            shape(heads, 2 * targets, sources, dtype=F32),
            [*values, reads],
            4 * targets * sources * heads * head_dim,
            1 << 21,
            [pltpu.VMEM((sources, groups * head_dim), BF16)],
        )

    scores = {"a": scored(distant), "b": scored(near)}

    def edges(name, shown):
        away, kept = kernel_call(
            functools.partial(edges_kernel, heads, queries, shown),
            (shape(2 * block, len(shown) * targets, dtype=F32),) * 2,
            [*tables, scores[name], direct, spots],
            len(shown) * targets * sources * sources * heads * 2,
            1 << 22,
        )
        away = swapped(away, "src", 1)
        back = swapped((kept[:block] + away[:block]).astype(BF16), "src", 2)
        cuts = [slice(i * targets, (i + 1) * targets) for i in range(len(shown))]
        return [
            kept[block:, cut] + away[block:, cut] + back[:, cut].astype(F32) for cut in cuts
        ]

    outer = edges("a", (2, 3))
    closer = edges("b", (0, 1))
    second = swapped(outer[0].astype(BF16), "tgt", 2)
    third = swapped(outer[1].astype(BF16), "tgt", 3)
    first = swapped(closer[1].astype(BF16), "tgt", 1)
    total = closer[0]
    for value in (first, second, third):
        total = total + value.astype(F32)
    return (total * cut[6]).astype(BF16)


def ring(
    target_rows, target_pos, decoder_rows, source_pos, out_proj, value_proj, attention, tile_pattern
):
    blocks = lax.axis_size("tgt")
    column = lax.axis_index("tgt")
    src_lane = lax.axis_index("src")
    full_targets, full_sources = (
        lax.all_gather(target_rows, "src", axis=0, tiled=True),
        lax.all_gather(decoder_rows, "src", axis=0, tiled=True),
    )
    tgt_dev = full_targets.shape[0]
    src_dev = full_sources.shape[0]
    sub_rows = decoder_rows.shape[0]
    heads_here = out_proj.shape[0]
    head_dim = out_proj.shape[2]
    groups_here = value_proj.shape[0]
    repeat = heads_here // groups_here
    read_sum = jnp.einsum(
        "td,hde->the",
        full_targets,
        lax.all_gather(out_proj, "tgt", axis=1, tiled=True),
        preferred_element_type=jnp.float32,
    )
    head_reads = read_sum.astype(jnp.bfloat16).reshape(tgt_dev, groups_here, repeat, head_dim)
    values = jnp.einsum("sd,gde->sge", full_sources, value_proj, preferred_element_type=jnp.float32)
    values = values.astype(jnp.bfloat16).reshape(src_dev, groups_here * head_dim)
    attn_table = lax.all_gather(attention, "tgt", axis=1, tiled=True)
    target_attn = jnp.take(attn_table, target_pos, axis=1)
    keyed_attn = jnp.transpose(target_attn, (0, 2, 1))

    def edge_tile(payload, block_index):
        decoder_part, value_part = payload
        key_positions = lax.dynamic_slice_in_dim(source_pos, block_index * src_dev, src_dev)
        weights = jnp.take(keyed_attn, key_positions, axis=1).astype(jnp.float32)
        scores = jnp.einsum(
            "sgd,tgrd->grst",
            value_part.reshape(src_dev, groups_here, head_dim),
            head_reads,
            preferred_element_type=jnp.float32,
        )
        scores = scores.reshape(heads_here, src_dev, tgt_dev)
        mixed_term = jnp.sum(weights * scores, axis=0)
        own_positions = lax.dynamic_slice_in_dim(key_positions, src_lane * sub_rows, sub_rows)
        same_place = (own_positions[:, None] == target_pos[None, :]).astype(jnp.float32)
        direct = (
            jnp.einsum("sd,td->st", decoder_part, full_targets, preferred_element_type=jnp.float32)
            * same_place
        )
        own_rows = lax.dynamic_slice_in_dim(mixed_term, src_lane * sub_rows, sub_rows, 0)
        return lax.dynamic_update_slice_in_dim(
            mixed_term, own_rows + direct, src_lane * sub_rows, 0
        )

    def place_tile(partial_value, payload, block_index):
        kept_flag = tile_pattern[block_index, column]
        piece_tile = edge_tile(payload, block_index) * kept_flag.astype(jnp.float32)
        return lax.dynamic_update_slice_in_dim(partial_value, piece_tile, block_index * src_dev, 0)

    own_block = (decoder_rows, values)
    partial_value = jnp.zeros((blocks * src_dev, tgt_dev), jnp.float32)
    partial_value = place_tile(partial_value, own_block, column)

    def cycle_turn(turn_index, state_carry):
        forward_block, backward_block, running = state_carry
        forward_block = passed_along((forward_block[0], forward_block[1]), "tgt", 1)
        backward_block = passed_along((backward_block[0], backward_block[1]), "tgt", -1)
        running = place_tile(running, forward_block, (column - turn_index) % blocks)
        running = place_tile(running, backward_block, (column + turn_index) % blocks)
        return (forward_block, backward_block, running)

    forward_block, _, partial_value = lax.fori_loop(
        1, blocks // 2, cycle_turn, (own_block, own_block, partial_value)
    )
    forward_block = passed_along((forward_block[0], forward_block[1]), "tgt", 1)
    partial_value = place_tile(partial_value, forward_block, (column - blocks // 2) % blocks)
    summed = lax.psum_scatter(partial_value, "src", scatter_dimension=0, tiled=True)
    return summed.astype(jnp.bfloat16)


def shards(*args):
    target_rows, target_pos, decoder_rows, source_pos, out_proj, value_proj, attention, _ = args
    blocks, lanes = lax.axis_size("tgt"), lax.axis_size("src")
    heads, groups = out_proj.shape[0], value_proj.shape[0]
    fits = (
        blocks == 4
        and lanes == 4
        and out_proj.shape[1] % 128 == 0
        and out_proj.shape[2] == 128
        and heads == 2 * groups
        and groups % 2 == 0
        and source_pos.shape[0] == target_pos.shape[0] == attention.shape[2] == 256
        and target_rows.shape[0] % 16 == 0
        and decoder_rows.shape[0] % 16 == 0
        and attention.shape[1] % 16 == 0
    )
    if not fits:
        return ring(*args)
    return resident(*args)


def solution(mesh):
    return jax.shard_map(
        shards,
        mesh=mesh,
        in_specs=(
            P(("grp", "tgt", "src"), None),
            P(("grp", "tgt")),
            P(("grp", "tgt", "src"), None),
            P("grp"),
            P("src", "tgt", None),
            P("src", None, None),
            P(("grp", "src"), "tgt", None),
            P("grp", None),
        ),
        out_specs=P(("grp", "src"), "tgt"),
        check_vma=False,
    )
```
